32 devices in a mesh: seq: 8 (over z, y), head: 4 (over x, core).
Axes of the slice: x: 2, y: 2, z: 4, core: 2. Of those that a mesh axis runs over, the one named last changes fastest.
Arguments:
- hidden: bfloat16 [4096, 8192], P('seq'), may hold values from -6 to 6
- w_query: bfloat16 [8192, 4096], P('seq', 'head'), may hold values from -0.0625 to 0.0625
- w_key: bfloat16 [8192, 4096], P('seq', 'head'), may hold values from -0.0625 to 0.0625
- w_value: bfloat16 [8192, 4096], P('seq', 'head'), may hold values from -0.0625 to 0.0625
- cotangent: bfloat16 [4096, 4096], P('seq', 'head'), may hold values from -6 to 6
Outputs:
- step_direction: float32 [4096, 8192], P(('seq', 'head'))
The draws below stay inside these ranges and needn't reach their ends.
All inputs are finite; a program needn't handle non-finite values.
Results may differ from the reference program's by a relative error of at most 0.015.
Values may be sent and summed in bfloat16 or wider, within the bound.
A program may use at most 192 MiB of HBM per device.

```python
import jax
import jax.numpy as jnp
from jax import lax

D = 8192
HEADS = 32
DH = 128
TOK_DEV = 512
TOKENS = 4096
N_HEAD = 4


def levels(key, extent, cuts, smallest, top_value):
    loudness = 1.0
    for dim, blocks in cuts:
        heights = jax.random.uniform(jax.random.fold_in(jax.random.fold_in(key, 6), dim), (blocks,), jnp.float32, smallest / len(cuts), top_value / len(cuts))
        loudness = loudness * jnp.repeat(jnp.exp(heights), extent[dim] // blocks).reshape((-1,) + (1,) * (len(extent) - 1 - dim))
    return loudness


def scatter_about(key, dims, spread, reach, split=(), dtype=jnp.bfloat16):
    drawn = spread * jax.random.normal(key, dims, jnp.float32)
    if split:
        drawn = drawn * levels(key, dims, split, -0.22, 0.18)
    return jnp.clip(drawn, -reach, reach).astype(dtype)


def setup_inputs(seed: int = 0) -> dict:
    keys = jax.random.split(jax.random.key(seed), 6)
    hidden = scatter_about(keys[0], (TOKENS, D), 1.0, 6.0, ((0, 8),))
    w_query = scatter_about(keys[1], (D, HEADS * DH), D ** -0.5, 0.0625, ((0, 8), (1, 4)))
    w_key = scatter_about(keys[2], (D, HEADS * DH), D ** -0.5, 0.0625, ((0, 8), (1, 4)))
    w_value = scatter_about(keys[3], (D, HEADS * DH), D ** -0.5, 0.0625, ((0, 8), (1, 4)))
    cotangent = scatter_about(keys[4], (TOKENS, HEADS * DH), 1.0, 6.0, ((0, 8), (1, 4)))
    return dict(hidden=hidden, w_query=w_query, w_key=w_key, w_value=w_value, cotangent=cotangent)


NORM_EPS = 1e-05
STEP_EPS = 1e-06

def silu_slope(preact):
    sigmoid = jax.nn.sigmoid(preact)
    return sigmoid * (1.0 + preact * (1.0 - sigmoid))

def reference(hidden, w_query, w_key, w_value, cotangent):
    col_total = w_query.shape[1]
    head_count = col_total // DH
    block_count = TOKENS // TOK_DEV
    pre_query = jnp.dot(hidden, w_query, preferred_element_type=jnp.float32)
    pre_key = jnp.dot(hidden, w_key, preferred_element_type=jnp.float32)
    pre_value = jnp.dot(hidden, w_value, preferred_element_type=jnp.float32)

    def blocked(matrix):
        return matrix.reshape(block_count, TOK_DEV, head_count, DH)
    query_rows = blocked(jax.nn.silu(pre_query).astype(jnp.bfloat16))
    key_rows = blocked(jax.nn.silu(pre_key).astype(jnp.bfloat16))
    value_rows = blocked(pre_value.astype(jnp.bfloat16))
    causal = (lax.broadcasted_iota(jnp.int32, (TOK_DEV, TOK_DEV), 0) >= lax.broadcasted_iota(jnp.int32, (TOK_DEV, TOK_DEV), 1))[None]

    def outer_sum(pair):
        return jnp.einsum('thi,thj->hij', pair[0].astype(jnp.float32), pair[1].astype(jnp.float32))
    own_states = lax.map(outer_sum, (key_rows, value_rows))
    zero_state = jnp.zeros_like(own_states[:1])
    before_all = jnp.concatenate([zero_state, jnp.cumsum(own_states, axis=0)[:-1]], axis=0)

    def block_scores(queries, keyed):
        scores = jnp.einsum('thd,shd->hts', queries.astype(jnp.float32), keyed.astype(jnp.float32))
        return jnp.where(causal, scores, 0.0).astype(jnp.bfloat16)

    def forward_block(parts):
        queries, keyed, valued, before = parts
        score_rows = block_scores(queries, keyed)
        inside = jnp.einsum('hts,shd->thd', score_rows.astype(jnp.float32), valued.astype(jnp.float32))
        carried = jnp.einsum('thi,hij->thj', queries.astype(jnp.float32), before, precision=lax.Precision.HIGHEST)
        return inside + carried
    attended = lax.map(forward_block, (query_rows, key_rows, value_rows, before_all))
    scale = lax.rsqrt(lax.optimization_barrier(jnp.mean(attended * attended, axis=-1, keepdims=True)) + NORM_EPS)
    normed = attended * scale
    upstream = blocked(cotangent.astype(jnp.float32))
    grad_att = (scale * (upstream - normed * lax.optimization_barrier(jnp.mean(upstream * normed, axis=-1, keepdims=True)))).astype(jnp.bfloat16)
    own_grads = lax.map(outer_sum, (query_rows, grad_att))
    inclusive = jnp.flip(jnp.cumsum(jnp.flip(own_grads, 0), axis=0), 0)
    after_all = jnp.concatenate([inclusive[1:], zero_state], axis=0)

    def backward_block(parts):
        queries, keyed, valued, grads, before, later_sum = parts
        score_rows = block_scores(queries, keyed).astype(jnp.float32)
        grad_scores = jnp.einsum('thd,shd->hts', grads.astype(jnp.float32), valued.astype(jnp.float32))
        grad_scores = jnp.where(causal, grad_scores, 0.0).astype(jnp.bfloat16).astype(jnp.float32)
        grad_query = jnp.einsum('hts,shd->thd', grad_scores, keyed.astype(jnp.float32)) + jnp.einsum('thj,hij->thi', grads.astype(jnp.float32), before, precision=lax.Precision.HIGHEST)
        grad_key = jnp.einsum('hts,thd->shd', grad_scores, queries.astype(jnp.float32)) + jnp.einsum('thj,hij->thi', valued.astype(jnp.float32), later_sum, precision=lax.Precision.HIGHEST)
        grad_value = jnp.einsum('hts,thd->shd', score_rows, grads.astype(jnp.float32)) + jnp.einsum('thi,hij->thj', keyed.astype(jnp.float32), later_sum, precision=lax.Precision.HIGHEST)
        return (grad_query, grad_key, grad_value)
    grad_query, grad_key, grad_value = lax.map(backward_block, (query_rows, key_rows, value_rows, grad_att, before_all, after_all))
    back_query = (grad_query.reshape(TOKENS, col_total) * silu_slope(pre_query)).astype(jnp.bfloat16)
    back_key = (grad_key.reshape(TOKENS, col_total) * silu_slope(pre_key)).astype(jnp.bfloat16)
    back_value = grad_value.reshape(TOKENS, col_total).astype(jnp.bfloat16)
    group_width = col_total // N_HEAD
    contract = (((1,), (1,)), ((), ()))
    input_grad = jnp.zeros((TOKENS, w_query.shape[0]), jnp.float32)
    for column_group in range(N_HEAD):
        columns = slice(column_group * group_width, (column_group + 1) * group_width)
        partial_value = lax.dot_general(back_query[:, columns], w_query[:, columns], contract, preferred_element_type=jnp.float32)
        partial_value = partial_value + lax.dot_general(back_key[:, columns], w_key[:, columns], contract, preferred_element_type=jnp.float32)
        partial_value = partial_value + lax.dot_general(back_value[:, columns], w_value[:, columns], contract, preferred_element_type=jnp.float32)
        rounded = lax.optimization_barrier(partial_value.astype(jnp.bfloat16))
        input_grad = input_grad + rounded.astype(jnp.float32)
    factor = lax.rsqrt(lax.optimization_barrier(jnp.mean(input_grad * input_grad, axis=-1, keepdims=True)) + STEP_EPS)
    return jnp.tanh(input_grad * factor)
```

```python
import functools

import jax
import jax.numpy as jnp
from jax import lax
from jax.experimental import pallas as pl
from jax.experimental.pallas import tpu as pltpu
from jax.sharding import PartitionSpec as P

DH = 128
NORM_EPS = 1e-05
STEP_EPS = 1e-06


F32 = jnp.float32
BF16 = jnp.bfloat16
MESH = pl.DeviceIdType.MESH
VMEM_LIMIT = 64000 * 1024
ROW_CUTS = 2
LEAD = 2


def silu_slope(preact):
    sigmoid = jax.nn.sigmoid(preact)
    return sigmoid * (1.0 + preact * (1.0 - sigmoid))


def swap(value, axis, mask, size):
    return lax.ppermute(value, axis, [(i, i ^ mask) for i in range(size)])


def flip(index, mask):
    bit = 1
    while bit <= mask:
        if mask & bit:
            index = index + bit * (1 - 2 * ((index // bit) % 2))
        bit *= 2
    return index


def xor(left, right, size):
    total, bit = 0, 1
    while bit < size:
        total = total + bit * ((left // bit + right // bit) % 2)
        bit *= 2
    return total


def bits_below(top):
    masks, bit = [], 1
    while bit < top:
        masks.append(bit)
        bit *= 2
    return masks


def greet(partners):
    barrier = pltpu.get_barrier_semaphore()
    for where in partners:
        pl.semaphore_signal(barrier, inc=1, device_id=where, device_id_type=MESH)
    pl.semaphore_wait(barrier, len(partners))


def gather_kernel(seq_count, head_parts, hidden, w_key, w_value, w_query, cot,
                  gathered, pre, cot_other, tokens, own, stage,
                  w_send, w_recv, tok_send, tok_recv, cot_sems, local, fetch):
    seat = lax.axis_index("seq")
    lane = lax.axis_index("head")
    tok_rows, _ = hidden.shape
    row_block, col_width = w_key.shape
    half = col_width // 2
    col_piece = stage.shape[2]
    row_piece = stage.shape[1]
    top, pair = seq_count // 2, seq_count // 4
    bit = (seat // pair) % 2
    low_masks = bits_below(pair)
    far_masks = (top | pair, top, pair)
    head_masks = bits_below(head_parts)
    share = tok_rows // head_parts
    weights = (w_key, w_value, w_query)
    pieces = [
        (proj, ch, r)
        for proj in range(3)
        for ch in range(half // col_piece)
        for r in range(row_block // row_piece)
    ]

    def seq_id(mask):
        return (flip(seat, mask), lane)

    def head_id(mask):
        return (seat, flip(lane, mask))

    greet([seq_id(m) for m in far_masks] + [seq_id(m) for m in low_masks]
          + [head_id(m) for m in head_masks])

    def remote(src, dst, send, recv, where):
        return pltpu.make_async_remote_copy(
            src_ref=src, dst_ref=dst, send_sem=send, recv_sem=recv,
            device_id=where, device_id_type=MESH,
        )

    def held(mask, p):
        proj, ch, r = pieces[p]
        return gathered.at[
            mask, pl.ds(r * row_piece, row_piece), pl.ds(proj * half + ch * col_piece, col_piece)
        ]

    def first_hop(mask, p):
        proj, ch, r = pieces[p]
        side = 1 - bit if mask & pair else bit
        column = pl.multiple_of(side * half + ch * col_piece, col_piece)
        src = weights[proj].at[pl.ds(r * row_piece, row_piece), pl.ds(column, col_piece)]
        return remote(src, held(mask, p), w_send.at[mask, p], w_recv.at[mask, p], seq_id(mask))

    def later_hop(mask, low, p):
        return remote(held(mask, p), held(mask ^ low, p), w_send.at[mask ^ low, p],
                      w_recv.at[mask ^ low, p], seq_id(low))

    def tok_rows_of(index, who):
        return tokens.at[index, pl.ds(pl.multiple_of(who * share, share), share)]

    tok_in = remote(
        hidden.at[pl.ds(pl.multiple_of(lane * share, share), share)], tok_rows_of(bit, lane),
        tok_send.at[0], tok_recv.at[0], seq_id(pair),
    )
    tok_in.start()
    sends = []
    for p in range(len(pieces)):
        for mask in low_masks:
            copy = first_hop(mask, p)
            copy.start()
            sends.append(copy)
    for p in range(-LEAD, len(pieces)):
        if p + LEAD < len(pieces):
            copy = first_hop(pair, p + LEAD)
            copy.start()
            sends.append(copy)
        if p >= 0:
            for mask in (top | pair, top):
                copy = first_hop(mask, p)
                copy.start()
                sends.append(copy)
        if p == -LEAD:
            side = pl.multiple_of((1 - bit) * half, half)
            cot_copy = remote(cot.at[:, pl.ds(side, half)], cot_other,
                              cot_sems.at[0], cot_sems.at[1], seq_id(pair))
            cot_copy.start()

    own_copies = []
    for proj in range(3):
        copy = pltpu.make_async_copy(
            weights[proj].at[:, pl.ds(pl.multiple_of(bit * half, half), half)],
            own.at[:, pl.ds(proj * half, half)], local.at[proj])
        copy.start()
        own_copies.append(copy)
    tok_local = pltpu.make_async_copy(hidden, tokens.at[bit], local.at[3])
    tok_local.start()
    for copy in own_copies:
        copy.wait()
    own_out = pltpu.make_async_copy(own, gathered.at[0], local.at[4])
    own_out.start()
    own_out.wait()
    tok_local.wait()

    def wait_recv(mask, p):
        here = held(mask, p)
        remote(here, here, w_send.at[mask, p], w_recv.at[mask, p], seq_id(pair)).wait_recv()

    arrived = set()

    def ensure(mask, p):
        if (mask, p) not in arrived:
            arrived.add((mask, p))
            wait_recv(mask, p)

    def spread(base, p):
        for low in low_masks:
            for sub in range(low):
                if base | sub:
                    ensure(base | sub, p)
                    copy = later_hop(base | sub, low, p)
                    copy.start()
                    sends.append(copy)

    def passes(p):
        for q in range(LEAD) if p == 0 else ():
            spread(pair, q)
        if p + LEAD < len(pieces):
            spread(pair, p + LEAD)
        spread(top | pair, p)
        spread(top, p)
        spread(0, p)

    def token_hop(step, mask, carried):
        copies = []
        for k, sub in enumerate(carried):
            block = tok_rows_of(1 - bit, flip(lane, sub))
            copy = remote(block, block, tok_send.at[step + k], tok_recv.at[step + k],
                          head_id(mask))
            copy.start()
            copies.append(copy)
        return copies

    hops = list(reversed(head_masks))
    carried = [0]

    def project(p):
        proj, ch, r = pieces[p]
        for mask in range(1, seq_count):
            ensure(mask, p)
        copies = []
        for mask in range(seq_count):
            copy = pltpu.make_async_copy(held(mask, p), stage.at[mask], fetch.at[mask])
            copy.start()
            copies.append(copy)
        for copy in copies:
            copy.wait()
        columns = pl.ds(ch * col_piece, col_piece)

        def block_dot(mask, carry):
            block = xor(seat, mask, seq_count)
            offset = pl.multiple_of(block * row_block + r * row_piece, row_piece)
            for side in range(2):
                term = jnp.dot(tokens[side, :, pl.ds(offset, row_piece)], stage[mask],
                               preferred_element_type=F32)
                pre[proj, side, :, columns] += term
            return carry

        if r == 0:
            for side in range(2):
                pre[proj, side, :, columns] = jnp.zeros((tok_rows, col_piece), F32)
        lax.fori_loop(0, seq_count, block_dot, 0)

    tok_copies = [tok_in]
    hops = list(reversed(head_masks))

    carried, flight, hop = [0], [tok_in], 0
    pending = []
    for p in range(len(pieces)):
        passes(p)
        pending.append(p)
        while hop <= len(hops) and (p >= 2 * hop + 1 or p == len(pieces) - 1):
            for copy in flight:
                copy.wait_recv()
            if hop < len(hops):
                flight = token_hop(len(tok_copies), hops[hop], carried)
                tok_copies += flight
                carried = carried + [c ^ hops[hop] for c in carried]
            hop += 1
        if hop > len(hops):
            for q in pending:
                project(q)
            pending = []
    for copy in sends:
        copy.wait_send()
    for copy in tok_copies:
        copy.wait_send()
    cot_copy.wait()


def gather_project(seq_count, head_parts, hidden, w_query, w_key, w_value, cotangent):
    tok_rows, width = hidden.shape
    row_block, col_width = w_query.shape
    half = col_width // 2
    col_piece = min(half, 256)
    row_piece = row_block // ROW_CUTS
    n_pieces = 3 * (half // col_piece) * ROW_CUTS
    anyspace = pl.BlockSpec(memory_space=pl.ANY)
    return pl.pallas_call(
        functools.partial(gather_kernel, seq_count, head_parts),
        name="gather_project",
        out_shape=(
            jax.ShapeDtypeStruct((seq_count, row_block, 3 * half), BF16),
            jax.ShapeDtypeStruct((3, 2, tok_rows, half), F32),
            jax.ShapeDtypeStruct((tok_rows, half), BF16),
        ),
        in_specs=[anyspace] * 5,
        out_specs=(anyspace, pl.BlockSpec(memory_space=pltpu.VMEM), anyspace),
        scratch_shapes=[
            pltpu.VMEM((2, tok_rows, width), BF16),
            pltpu.VMEM((row_block, 3 * half), BF16),
            pltpu.VMEM((seq_count, row_piece, col_piece), BF16),
            pltpu.SemaphoreType.DMA((seq_count, n_pieces)),
            pltpu.SemaphoreType.DMA((seq_count, n_pieces)),
            pltpu.SemaphoreType.DMA((head_parts,)),
            pltpu.SemaphoreType.DMA((head_parts,)),
            pltpu.SemaphoreType.DMA((2,)),
            pltpu.SemaphoreType.DMA((5,)),
            pltpu.SemaphoreType.DMA((seq_count,)),
        ],
        compiler_params=pltpu.CompilerParams(
            collective_id=0, has_side_effects=True, vmem_limit_bytes=VMEM_LIMIT
        ),
    )(hidden, w_key, w_value, w_query, cotangent)


def reduce_kernel(seq_count, head_parts, kt, lag, back, gathered, out, *scratch):
    seat = lax.axis_index("seq")
    lane = lax.axis_index("head")
    out_rows = back.shape[1]
    row_block, _ = gathered.shape[1:]
    per_block = row_block // kt
    n_tiles = seq_count * per_block
    pair = seq_count // 4
    bit = (seat // pair) % 2
    head_masks = bits_below(head_parts)
    nd = len(head_masks) + 1
    groups = 2 ** nd
    dims = [((seat, flip(lane, m)), nd - 1 - k) for k, m in enumerate(head_masks)]
    dims.append(((flip(seat, pair), lane), 0))
    orders = (
        list(range(nd)),
        [0, nd - 1] + list(range(1, nd - 1)),
    )
    rel, w_slots = scratch[0], scratch[1]
    keeps = scratch[2:2 + nd]
    send_bufs = scratch[2 + nd:2 + 2 * nd]
    recv_bufs = scratch[2 + 2 * nd:2 + 3 * nd]
    w_sem, send_sem, recv_sem = scratch[2 + 3 * nd:]

    greet([where for where, _ in dims])

    base = seat - bit * pair

    def fetch(j):
        block = xor(j // per_block, bit * pair, seq_count)
        row = pl.multiple_of((j % per_block) * kt, kt)
        return pltpu.make_async_copy(
            gathered.at[block, pl.ds(row, kt)], w_slots.at[j % 2], w_sem.at[j % 2])

    fetch(0).start()
    for g in range(groups):
        far_side = g % 2
        who = lane
        for k, m in enumerate(head_masks):
            if (g >> (nd - 1 - k)) & 1:
                who = flip(who, m)
        side = flip(bit, 1) if far_side else bit
        rel[pl.ds(g * out_rows, out_rows)] = back[side * head_parts + who]

    plans = []
    for order in orders:
        plan, current = [], list(range(groups))
        for d in order:
            place = dims[d][1]
            sent = [i for i, g in enumerate(current) if (g >> place) & 1]
            kept = [i for i, g in enumerate(current) if not (g >> place) & 1]
            plan.append((d, sent, kept))
            current = [current[i] for i in kept]
        plans.append(plan)

    def copy_of(stage, tile, where):
        return pltpu.make_async_remote_copy(
            src_ref=send_bufs[stage].at[tile], dst_ref=recv_bufs[stage].at[tile],
            send_sem=send_sem.at[stage, tile], recv_sem=recv_sem.at[stage, tile],
            device_id=where, device_id_type=MESH)

    rows_half = groups // 2 * out_rows

    def multiply(j, plan):
        fetch(j).wait()

        @pl.when(j + 1 < n_tiles)
        def _():
            fetch(j + 1).start()

        w = w_slots[j % 2]
        contract = (((1,), (1,)), ((), ()))
        away = lax.dot_general(rel[pl.ds(rows_half, rows_half)], w, contract,
                               preferred_element_type=F32)
        send_bufs[0][j] = away.astype(BF16).reshape(groups // 2, out_rows, kt)
        copy_of(0, j, dims[plan[0][0]][0]).start()
        home = lax.dot_general(rel[pl.ds(0, rows_half)], w, contract, preferred_element_type=F32)
        keeps[0][j % keeps[0].shape[0]] = home.reshape(groups // 2, out_rows, kt)

    def forward(stage, j, plan):
        copy_of(stage - 1, j, dims[plan[stage - 1][0]][0]).wait_recv()
        slot = j % keeps[stage - 1].shape[0]
        if stage == nd:
            total = keeps[stage - 1][slot, 0] + recv_bufs[stage - 1][j, 0].astype(F32)
            block = xor(base, j // per_block, seq_count)
            column = pl.multiple_of(block * row_block + (j % per_block) * kt, kt)
            out[:, pl.ds(column, kt)] = total
            return
        d, sent, kept = plan[stage]
        for k, i in enumerate(sent):
            total = keeps[stage - 1][slot, i] + recv_bufs[stage - 1][j, i].astype(F32)
            send_bufs[stage][j, k] = total.astype(BF16)
        copy_of(stage, j, dims[d][0]).start()
        here = j % keeps[stage].shape[0]
        for k, i in enumerate(kept):
            keeps[stage][here, k] = keeps[stage - 1][slot, i] + recv_bufs[stage - 1][j, i].astype(F32)

    delays = [0] + [1 + lag * s for s in range(nd)]
    steps = n_tiles + delays[-1]

    def step(i, carry):
        for parity in range(2):
            now = i * 2 + parity

            @pl.when(now < n_tiles)
            def _():
                multiply(now, plans[parity])

            for stage in range(1, nd + 1):
                j = now - delays[stage]
                plan = plans[(parity - delays[stage]) % 2]

                @pl.when((j >= 0) & (j < n_tiles))
                def _():
                    forward(stage, j, plan)
        return carry

    lax.fori_loop(0, (steps + 1) // 2, step, 0)

    def drain(j, carry):
        for stage in range(nd):
            copy_of(stage, j, dims[0][0]).wait_send()
        return carry

    lax.fori_loop(0, n_tiles, drain, 0)


def project_back(seq_count, head_parts, back, gathered):
    groups, out_rows, depth = back.shape
    row_block = gathered.shape[1]
    kt = row_block // 2
    n_tiles = seq_count * 2
    lag = 3
    nd = len(bits_below(head_parts)) + 1
    sizes = [groups >> (s + 1) for s in range(nd)]
    return pl.pallas_call(
        functools.partial(reduce_kernel, seq_count, head_parts, kt, lag),
        name="project_back",
        out_shape=jax.ShapeDtypeStruct((out_rows, seq_count * row_block), F32),
        in_specs=[pl.BlockSpec(memory_space=pltpu.VMEM), pl.BlockSpec(memory_space=pl.ANY)],
        out_specs=pl.BlockSpec(memory_space=pltpu.VMEM),
        scratch_shapes=[
            pltpu.VMEM((groups * out_rows, depth), BF16),
            pltpu.VMEM((2, kt, depth), BF16),
            *[pltpu.VMEM((2 if s == 0 else lag + 1, n, out_rows, kt), F32)
              for s, n in enumerate(sizes)],
            *[pltpu.VMEM((n_tiles, n, out_rows, kt), BF16) for n in sizes],
            *[pltpu.VMEM((n_tiles, n, out_rows, kt), BF16) for n in sizes],
            pltpu.SemaphoreType.DMA((2,)),
            pltpu.SemaphoreType.DMA((nd, n_tiles)),
            pltpu.SemaphoreType.DMA((nd, n_tiles)),
        ],
        compiler_params=pltpu.CompilerParams(
            collective_id=1, has_side_effects=True, vmem_limit_bytes=VMEM_LIMIT
        ),
    )(back, gathered)


def scan_states(own, seq_count, later):
    seat = lax.axis_index("seq")
    top, pair = seq_count // 2, seq_count // 4
    total = own
    outside = jnp.zeros_like(own)
    for mask in bits_below(pair):
        other = swap(total.astype(BF16), "seq", mask, seq_count).astype(F32)
        wanted = (seat & mask) == (0 if later else mask)
        outside = outside + jnp.where(wanted, other, 0.0)
        total = total + other
    if later:
        outside = outside.at[0].add(total[1])
    else:
        outside = outside.at[1].add(total[0])
    whole = total[0] + total[1]
    other = swap(whole.astype(BF16), "seq", top, seq_count).astype(F32)
    wanted = (seat & top) == (0 if later else top)
    return outside + jnp.where(wanted, other, 0.0)[None]


def attend(seq_count, pre, cot):
    _, _, tok_rows, cols = pre.shape
    shape = (2, tok_rows, cols // DH, DH)
    pre_key, pre_value, pre_query = (pre[i].reshape(shape) for i in range(3))
    key_rows = jax.nn.silu(pre_key).astype(BF16)
    value_rows = pre_value.astype(BF16)
    query_rows = jax.nn.silu(pre_query).astype(BF16)
    own_state = jnp.einsum("bthi,bthj->bhij", key_rows, value_rows, preferred_element_type=F32)
    before = scan_states(own_state, seq_count, False)
    causal = (
        lax.broadcasted_iota(jnp.int32, (tok_rows, tok_rows), 0)
        >= lax.broadcasted_iota(jnp.int32, (tok_rows, tok_rows), 1)
    )[None, None]
    scores = jnp.einsum("bthd,bshd->bhts", query_rows, key_rows, preferred_element_type=F32)
    score_rows = jnp.where(causal, scores, 0.0).astype(BF16)
    inside = jnp.einsum("bhts,bshd->bthd", score_rows, value_rows, preferred_element_type=F32)
    carried = jnp.einsum(
        "bthi,bhij->bthj", query_rows.astype(F32), before, precision=lax.Precision.HIGHEST
    )
    attended = inside + carried
    scale = lax.rsqrt(jnp.mean(attended * attended, axis=-1, keepdims=True) + NORM_EPS)
    normed = attended * scale
    upstream = cot.astype(F32).reshape(shape)
    grad_att = (
        scale * (upstream - normed * jnp.mean(upstream * normed, axis=-1, keepdims=True))
    ).astype(BF16)
    own_grad = jnp.einsum("bthi,bthj->bhij", query_rows, grad_att, preferred_element_type=F32)
    later_sum = scan_states(own_grad, seq_count, True)
    grad_scores = jnp.einsum("bthd,bshd->bhts", grad_att, value_rows, preferred_element_type=F32)
    grad_scores = jnp.where(causal, grad_scores, 0.0).astype(BF16)
    highest = lax.Precision.HIGHEST
    grad_query = jnp.einsum(
        "bhts,bshd->bthd", grad_scores, key_rows, preferred_element_type=F32
    ) + jnp.einsum("bthj,bhij->bthi", grad_att.astype(F32), before, precision=highest)
    grad_key = jnp.einsum(
        "bhts,bthd->bshd", grad_scores, query_rows, preferred_element_type=F32
    ) + jnp.einsum("bthj,bhij->bthi", value_rows.astype(F32), later_sum, precision=highest)
    grad_value = jnp.einsum(
        "bhts,bthd->bshd", score_rows, grad_att, preferred_element_type=F32
    ) + jnp.einsum("bthi,bhij->bthj", key_rows.astype(F32), later_sum, precision=highest)
    back_key = (grad_key * silu_slope(pre_key)).astype(BF16)
    back_value = grad_value.astype(BF16)
    back_query = (grad_query * silu_slope(pre_query)).astype(BF16)
    return jnp.concatenate(
        [b.reshape(2, tok_rows, cols) for b in (back_key, back_value, back_query)], axis=2
    )


def on_device(seq_count, head_parts, hidden, w_query, w_key, w_value, cotangent):
    tok_rows, _ = hidden.shape
    half = w_query.shape[1] // 2
    seat = lax.axis_index("seq")
    bit = (seat // (seq_count // 4)) % 2
    gathered, pre, cot_other = gather_project(
        seq_count, head_parts, hidden, w_query, w_key, w_value, cotangent
    )
    cot_own = lax.dynamic_slice_in_dim(cotangent, bit * half, half, 1)
    cot = jnp.where(
        bit == 0, jnp.stack([cot_own, cot_other]), jnp.stack([cot_other, cot_own])
    )
    back = attend(seq_count, pre, cot)
    back = back.reshape(2 * head_parts, tok_rows // head_parts, 3 * half)
    input_grad = project_back(seq_count, head_parts, back, gathered)
    factor = lax.rsqrt(jnp.mean(input_grad * input_grad, axis=-1, keepdims=True) + STEP_EPS)
    return jnp.tanh(input_grad * factor)


def solution(mesh):
    def body(*args):
        return on_device(mesh.shape["seq"], mesh.shape["head"], *args)

    return jax.shard_map(
        body,
        mesh=mesh,
        in_specs=(
            P("seq", None),
            P("seq", "head"),
            P("seq", "head"),
            P("seq", "head"),
            P("seq", "head"),
        ),
        out_specs=P(("seq", "head"), None),
        check_vma=False,
    )
```

```python
import functools

import jax
import jax.numpy as jnp
from jax import lax
from jax.experimental import pallas as pl
from jax.experimental.pallas import tpu as pltpu
from jax.sharding import PartitionSpec as P

DH = 128
NORM_EPS = 1e-05
STEP_EPS = 1e-06


F32 = jnp.float32
BF16 = jnp.bfloat16
MESH = pl.DeviceIdType.MESH
VMEM_LIMIT = 64000 * 1024
ROW_CUTS = 2
LAST_CUTS = (2, 1, 1)
AHEAD = 2
HELD_BACK = (2, 2)
TOP_GAP = 4
TOKEN_CUTS = 4
CATCH_UP = 4


def silu_slope(preact):
    sigmoid = jax.nn.sigmoid(preact)
    return sigmoid * (1.0 + preact * (1.0 - sigmoid))


def flip(index, mask):
    bit = 1
    while bit <= mask:
        if mask & bit:
            index = index + bit * (1 - 2 * ((index // bit) % 2))
        bit *= 2
    return index


def xor(left, right, size):
    total, bit = 0, 1
    while bit < size:
        total = total + bit * ((left // bit + right // bit) % 2)
        bit *= 2
    return total


def bits_below(top):
    masks, bit = [], 1
    while bit < top:
        masks.append(bit)
        bit *= 2
    return masks


def cut_pieces(row_block, n_chunks):
    pieces = []
    for ch in range(n_chunks):
        for proj in range(3):
            last = ch == n_chunks - 1 and proj == 2
            row = 0
            for share in LAST_CUTS if last else (2,) * ROW_CUTS:
                rows = row_block // ROW_CUTS // 2 * share
                pieces.append((proj, ch, row, rows))
                row += rows
    return pieces


def greet(partners):
    barrier = pltpu.get_barrier_semaphore()
    for where in partners:
        pl.semaphore_signal(barrier, inc=1, device_id=where, device_id_type=MESH)
    pl.semaphore_wait(barrier, len(partners))


def layer_kernel(seq_count, head_parts, hidden, w_key, w_value, w_query, cot,
                 gathered, back, tokens, own, stage, pre, act, scores, grads, cot_rows,
                 outside, total, low_send, low_recv, top_send, top_recv,
                 w_send, w_recv, tok_send, tok_recv, cot_sems, local, fetch,
                 low_sems, top_sems):
    seat = lax.axis_index("seq")
    lane = lax.axis_index("head")
    tok_rows, _ = hidden.shape
    row_block, col_width = w_key.shape
    half = col_width // 2
    _, col_piece = stage.shape[1:]
    top, pair = seq_count // 2, seq_count // 4
    bit = (seat // pair) % 2
    low_masks = bits_below(pair)
    far_masks = (top | pair, top, pair)
    head_masks = bits_below(head_parts)
    share = tok_rows // head_parts
    weights = (w_key, w_value, w_query)
    n_chunks = half // col_piece
    chunk_heads = col_piece // DH
    pieces = cut_pieces(row_block, n_chunks)

    def seq_id(mask):
        return (flip(seat, mask), lane)

    def head_id(mask):
        return (seat, flip(lane, mask))

    greet([seq_id(m) for m in far_masks] + [seq_id(m) for m in low_masks]
          + [head_id(m) for m in head_masks])

    def remote(src, dst, send, recv, where):
        return pltpu.make_async_remote_copy(
            src_ref=src, dst_ref=dst, send_sem=send, recv_sem=recv,
            device_id=where, device_id_type=MESH,
        )

    sends = []

    def start(copy):
        copy.start()
        sends.append(copy)
        return copy


    def held(mask, p):
        proj, ch, row, rows = pieces[p]
        return gathered.at[
            mask, pl.ds(row, rows), pl.ds(proj * half + ch * col_piece, col_piece)
        ]

    def first_hop(mask, p):
        proj, ch, row, rows = pieces[p]
        side = 1 - bit if mask & pair else bit
        column = pl.multiple_of(side * half + ch * col_piece, col_piece)
        src = weights[proj].at[pl.ds(row, rows), pl.ds(column, col_piece)]
        return remote(src, held(mask, p), w_send.at[mask, p], w_recv.at[mask, p], seq_id(mask))

    def later_hop(mask, low, p):
        return remote(held(mask, p), held(mask | low, p), w_send.at[mask | low, p],
                      w_recv.at[mask | low, p], seq_id(low))

    arrived = set()

    def ensure(mask, p):
        if (mask, p) not in arrived:
            arrived.add((mask, p))
            here = held(mask, p)
            remote(here, here, w_send.at[mask, p], w_recv.at[mask, p], seq_id(pair)).wait_recv()

    def spread(base, p):
        for low in low_masks:
            for sub in range(low):
                if base | sub:
                    ensure(base | sub, p)
                    start(later_hop(base | sub, low, p))


    slab = share // TOKEN_CUTS
    hops = list(reversed(head_masks))

    def tok_block(index, who, cut):
        row = pl.multiple_of(who * share + cut * slab, slab)
        return tokens.at[index, pl.ds(row, slab)]

    def token_first(cut):
        row = pl.multiple_of(lane * share + cut * slab, slab)
        return remote(hidden.at[pl.ds(row, slab)], tok_block(bit, lane, cut),
                      tok_send.at[cut, 0], tok_recv.at[cut, 0], seq_id(pair))

    flights = {}

    def token_hop(cut, hop):
        for copy in flights[cut]:
            copy.wait_recv()
        if hop < len(hops):
            count = 2 ** hop
            held_shares = [0]
            for mask in hops[:hop]:
                held_shares = held_shares + [c ^ mask for c in held_shares]
            flights[cut] = []
            for k, sub in enumerate(held_shares):
                block = tok_block(1 - bit, flip(lane, sub), cut)
                flights[cut].append(start(remote(
                    block, block, tok_send.at[cut, count + k], tok_recv.at[cut, count + k],
                    head_id(hops[hop]))))

    side = pl.multiple_of((1 - bit) * half, half)
    cot_copy = remote(cot.at[:, pl.ds(side, half)], cot_rows.at[bit],
                      cot_sems.at[0], cot_sems.at[1], seq_id(pair))

    def issue(p):
        for mask in (top | pair, top, pair):
            start(first_hop(mask, p))
        for mask in low_masks:
            start(first_hop(mask, p))
        for cut in range(TOKEN_CUTS):
            if cut // 2 == p:
                flights[cut] = [start(token_first(cut))]
        if p == TOKEN_CUTS:
            start(cot_copy)

    issued = [0]

    def issue_to(count):
        while issued[0] < min(count, len(pieces)):
            issue(issued[0])
            issued[0] += 1

    issue_to(len(pieces) - HELD_BACK[0] if n_chunks > 1 else len(pieces))

    mine = pl.multiple_of(bit * half, half)
    own_copies = []
    for proj in range(3):
        copy = pltpu.make_async_copy(weights[proj].at[:, pl.ds(mine, half)],
                                     own.at[:, pl.ds(proj * half, half)], local.at[proj])
        copy.start()
        own_copies.append(copy)
    tok_local = pltpu.make_async_copy(hidden, tokens.at[bit], local.at[3])
    tok_local.start()
    cot_local = pltpu.make_async_copy(cot.at[:, pl.ds(mine, half)], cot_rows.at[bit], local.at[5])
    for copy in own_copies:
        copy.wait()
    own_out = pltpu.make_async_copy(own, gathered.at[0], local.at[4])
    own_out.start()
    own_out.wait()
    tok_local.wait()

    def project(p):
        proj, ch, row, rows = pieces[p]
        for mask in range(1, seq_count):
            ensure(mask, p)
        copies = []
        for mask in range(seq_count):
            copy = pltpu.make_async_copy(
                held(mask, p), stage.at[mask, pl.ds(0, rows)], fetch.at[mask])
            copy.start()
            copies.append(copy)
        for copy in copies:
            copy.wait()
        columns = pl.ds(ch * col_piece, col_piece)

        def block_dot(mask, carry):
            block = xor(seat, mask, seq_count)
            offset = pl.multiple_of(block * row_block + row, DH)
            for side in range(2):
                term = jnp.dot(tokens[side, :, pl.ds(offset, rows)], stage[mask, pl.ds(0, rows)],
                               preferred_element_type=F32)
                pre[proj, side, :, columns] += term
            return carry

        if row == 0:
            for side in range(2):
                pre[proj, side, :, columns] = jnp.zeros((tok_rows, col_piece), F32)
        lax.fori_loop(0, seq_count, block_dot, 0)


    def per_item(ch, work):
        def item(i, carry):
            head = ch * chunk_heads + i % chunk_heads
            work(i // chunk_heads, head, pl.ds(pl.multiple_of(head * DH, DH), DH))
            return carry

        lax.fori_loop(0, 2 * chunk_heads, item, 0)

    causal = (
        lax.broadcasted_iota(jnp.int32, (tok_rows, tok_rows), 0)
        >= lax.broadcasted_iota(jnp.int32, (tok_rows, tok_rows), 1)
    )

    def dot(left, right, left_dim, right_dim):
        return lax.dot_general(left, right, (((left_dim,), (right_dim,)), ((), ())),
                               preferred_element_type=F32)

    def states(side, head, cols):
        key = jax.nn.silu(pre[0, side, :, cols]).astype(BF16)
        value = pre[1, side, :, cols].astype(BF16)
        act[0, side, :, cols] = key
        act[1, side, :, cols] = value
        total[0, side, head] = dot(key, value, 0, 0)
        outside[0, side, head] = jnp.zeros((DH, DH), F32)

    def forward(side, head, cols):
        query = jax.nn.silu(pre[2, side, :, cols]).astype(BF16)
        act[2, side, :, cols] = query
        key, value = act[0, side, :, cols], act[1, side, :, cols]
        masked = jnp.where(causal, dot(query, key, 1, 1), 0.0).astype(BF16)
        scores[side, head] = masked
        attended = dot(masked, value, 1, 0) + dot(query, outside[0, side, head].astype(BF16), 1, 0)
        scale = lax.rsqrt(jnp.mean(attended * attended, axis=-1, keepdims=True) + NORM_EPS)
        normed = attended * scale
        upstream = cot_rows[side, :, cols].astype(F32)
        grad = scale * (upstream - normed * jnp.mean(upstream * normed, axis=-1, keepdims=True))
        grad = grad.astype(BF16)
        grads[side, :, cols] = grad
        total[1, side, head] = dot(query, grad, 0, 0)
        outside[1, side, head] = jnp.zeros((DH, DH), F32)

    def backward(side, head, cols):
        key, value, query = (act[i, side, :, cols] for i in range(3))
        grad = grads[side, :, cols]
        before = outside[0, side, head].astype(BF16)
        after = outside[1, side, head].astype(BF16)
        grad_scores = jnp.where(causal, dot(grad, value, 1, 1), 0.0).astype(BF16)
        grad_query = dot(grad_scores, key, 1, 0) + dot(grad, before, 1, 1)
        grad_key = dot(grad_scores, query, 0, 0) + dot(value, after, 1, 1)
        grad_value = dot(scores[side, head], grad, 0, 0) + dot(key, after, 1, 0)
        results = (
            grad_key * silu_slope(pre[0, side, :, cols]),
            grad_value,
            grad_query * silu_slope(pre[2, side, :, cols]),
        )
        for proj, result in enumerate(results):
            column = pl.ds(pl.multiple_of(proj * half + head * DH, DH), DH)
            back[side, :, column] = result.astype(BF16)


    def heads_of(ch):
        return range(ch * chunk_heads, (ch + 1) * chunk_heads)

    def low_copy(kind, ch, i):
        return remote(low_send.at[kind, ch, i], low_recv.at[kind, ch, i],
                      low_sems.at[0, kind, ch, i], low_sems.at[1, kind, ch, i],
                      seq_id(low_masks[i]))

    def top_copy(kind, ch):
        return remote(top_send.at[kind, ch], top_recv.at[kind, ch],
                      top_sems.at[0, kind, ch], top_sems.at[1, kind, ch], seq_id(top))

    def scan_send(kind, ch, i):
        for side in range(2):
            for k, head in enumerate(heads_of(ch)):
                low_send[kind, ch, i, side, k] = total[kind, side, head].astype(BF16)
        start(low_copy(kind, ch, i))

    def scan_low(kind, ch):
        for i, low in enumerate(low_masks):
            low_copy(kind, ch, i).wait_recv()
            wanted = (seat // low) % 2 == 1 - kind
            for side in range(2):
                for k, head in enumerate(heads_of(ch)):
                    other = low_recv[kind, ch, i, side, k].astype(F32)
                    outside[kind, side, head] += jnp.where(wanted, other, 0.0)
                    total[kind, side, head] += other
            if i + 1 < len(low_masks):
                scan_send(kind, ch, i + 1)
        for k, head in enumerate(heads_of(ch)):
            outside[kind, 1 - kind, head] += total[kind, kind, head]
            whole = total[kind, 0, head] + total[kind, 1, head]
            top_send[kind, ch, k] = whole.astype(BF16)
        start(top_copy(kind, ch))

    def scan_top(kind, ch):
        top_copy(kind, ch).wait_recv()
        wanted = (seat // top) % 2 == 1 - kind
        for k, head in enumerate(heads_of(ch)):
            other = jnp.where(wanted, top_recv[kind, ch, k].astype(F32), 0.0)
            for side in range(2):
                outside[kind, side, head] += other

    def stage_states(ch):
        per_item(ch, states)
        scan_send(0, ch, 0)

    def stage_forward(ch):
        per_item(ch, forward)
        scan_send(1, ch, 0)

    chain = (
        (stage_states, 2, 0),
        (lambda ch: scan_low(0, ch), 2, 1),
        (lambda ch: scan_top(0, ch), 2, TOP_GAP),
        (stage_forward, 3, 0),
        (lambda ch: scan_low(1, ch), 3, 1),
        (lambda ch: scan_top(1, ch), 3, TOP_GAP),
        (lambda ch: per_item(ch, backward), 3, 0),
    )
    place = [0] * n_chunks
    last_step = [0] * n_chunks
    projected = [0] * n_chunks
    cot_here = []

    def advance(p, final):
        moved = True
        while moved:
            moved = False
            for ch in range(n_chunks):
                if place[ch] == len(chain):
                    continue
                work, projs, gap = chain[place[ch]]
                if projected[ch] < projs * row_block or not (final or p >= last_step[ch] + gap):
                    continue
                if work is stage_forward and not cot_here:
                    cot_here.append(True)
                    cot_copy.wait_recv()
                    cot_local.start()
                    cot_local.wait()
                work(ch)
                place[ch] += 1
                if ch == 0 and place[ch] in (2, 5):
                    issue_to(len(pieces) - HELD_BACK[1] if place[ch] == 2 else len(pieces))
                last_step[ch] = p
                moved = True

    tok_step = (TOKEN_CUTS - 1) // 2 + 1 + len(hops)
    pending = []
    for p in range(len(pieces)):
        final = p == len(pieces) - 1
        issue_to(p + AHEAD)
        for mask in (top | pair, top, pair, 0):
            spread(mask, p)
        if final:
            pending.append(p)
        for hop in range(len(hops) + 1):
            for cut in range(TOKEN_CUTS):
                due = cut // 2 + 1 + hop
                if due == p or (final and due > p):
                    token_hop(cut, hop)
        if p >= tok_step or final:
            count = len(pending) if final else CATCH_UP
            for q in pending[:count]:
                project(q)
                projected[pieces[q][1]] += pieces[q][3]
                if final:
                    advance(p, True)
            pending = pending[count:]
            advance(p, final)
        pending.append(p)
    for copy in sends:
        copy.wait_send()


def layer(seq_count, head_parts, hidden, w_query, w_key, w_value, cotangent):
    tok_rows, width = hidden.shape
    row_block, col_width = w_query.shape
    half = col_width // 2
    heads = half // DH
    col_piece = min(half, 256)
    row_piece = row_block // ROW_CUTS
    n_chunks = half // col_piece
    chunk_heads = col_piece // DH
    n_pieces = len(cut_pieces(row_block, n_chunks))
    n_low = len(bits_below(seq_count // 4))
    anyspace = pl.BlockSpec(memory_space=pl.ANY)
    dma = pltpu.SemaphoreType.DMA
    return pl.pallas_call(
        functools.partial(layer_kernel, seq_count, head_parts),
        name="layer",
        out_shape=(
            jax.ShapeDtypeStruct((seq_count, row_block, 3 * half), BF16),
            jax.ShapeDtypeStruct((2, tok_rows, 3 * half), BF16),
        ),
        in_specs=[anyspace] * 5,
        out_specs=(anyspace, pl.BlockSpec(memory_space=pltpu.VMEM)),
        scratch_shapes=[
            pltpu.VMEM((2, tok_rows, width), BF16),
            pltpu.VMEM((row_block, 3 * half), BF16),
            pltpu.VMEM((seq_count, row_piece, col_piece), BF16),
            pltpu.VMEM((3, 2, tok_rows, half), F32),
            pltpu.VMEM((3, 2, tok_rows, half), BF16),
            pltpu.VMEM((2, heads, tok_rows, tok_rows), BF16),
            pltpu.VMEM((2, tok_rows, half), BF16),
            pltpu.VMEM((2, tok_rows, half), BF16),
            pltpu.VMEM((2, 2, heads, DH, DH), F32),
            pltpu.VMEM((2, 2, heads, DH, DH), F32),
            pltpu.VMEM((2, n_chunks, n_low, 2, chunk_heads, DH, DH), BF16),
            pltpu.VMEM((2, n_chunks, n_low, 2, chunk_heads, DH, DH), BF16),
            pltpu.VMEM((2, n_chunks, chunk_heads, DH, DH), BF16),
            pltpu.VMEM((2, n_chunks, chunk_heads, DH, DH), BF16),
            dma((seq_count, n_pieces)),
            dma((seq_count, n_pieces)),
            dma((TOKEN_CUTS, head_parts)),
            dma((TOKEN_CUTS, head_parts)),
            dma((2,)),
            dma((6,)),
            dma((seq_count,)),
            dma((2, 2, n_chunks, n_low)),
            dma((2, 2, n_chunks)),
        ],
        compiler_params=pltpu.CompilerParams(
            collective_id=0, has_side_effects=True, vmem_limit_bytes=VMEM_LIMIT
        ),
    )(hidden, w_key, w_value, w_query, cotangent)


def reduce_kernel(seq_count, head_parts, kt, lag, back, gathered, out, *scratch):
    seat = lax.axis_index("seq")
    lane = lax.axis_index("head")
    out_rows = back.shape[1]
    row_block, _ = gathered.shape[1:]
    per_block = row_block // kt
    n_tiles = seq_count * per_block
    pair = seq_count // 4
    bit = (seat // pair) % 2
    head_masks = bits_below(head_parts)
    nd = len(head_masks) + 1
    groups = 2 ** nd
    dims = [((seat, flip(lane, m)), nd - 1 - k) for k, m in enumerate(head_masks)]
    dims.append(((flip(seat, pair), lane), 0))
    orders = (
        list(range(nd)),
        [0, nd - 1] + list(range(1, nd - 1)),
    )
    rel, w_slots = scratch[0], scratch[1]
    keeps = scratch[2:2 + nd]
    send_bufs = scratch[2 + nd:2 + 2 * nd]
    recv_bufs = scratch[2 + 2 * nd:2 + 3 * nd]
    w_sem, send_sem, recv_sem = scratch[2 + 3 * nd:]

    greet([where for where, _ in dims])

    base = seat - bit * pair

    def fetch(j):
        block = xor(j // per_block, bit * pair, seq_count)
        row = pl.multiple_of((j % per_block) * kt, kt)
        return pltpu.make_async_copy(
            gathered.at[block, pl.ds(row, kt)], w_slots.at[j % 2], w_sem.at[j % 2])

    fetch(0).start()
    for g in range(groups):
        far_side = g % 2
        who = lane
        for k, m in enumerate(head_masks):
            if (g >> (nd - 1 - k)) & 1:
                who = flip(who, m)
        side = flip(bit, 1) if far_side else bit
        rel[pl.ds(g * out_rows, out_rows)] = back[side * head_parts + who]

    plans = []
    for order in orders:
        plan, current = [], list(range(groups))
        for d in order:
            place = dims[d][1]
            sent = [i for i, g in enumerate(current) if (g >> place) & 1]
            kept = [i for i, g in enumerate(current) if not (g >> place) & 1]
            plan.append((d, sent, kept))
            current = [current[i] for i in kept]
        plans.append(plan)

    def copy_of(stage, tile, where):
        return pltpu.make_async_remote_copy(
            src_ref=send_bufs[stage].at[tile], dst_ref=recv_bufs[stage].at[tile],
            send_sem=send_sem.at[stage, tile], recv_sem=recv_sem.at[stage, tile],
            device_id=where, device_id_type=MESH)

    rows_half = groups // 2 * out_rows

    def multiply(j, plan):
        fetch(j).wait()

        @pl.when(j + 1 < n_tiles)
        def _():
            fetch(j + 1).start()

        w = w_slots[j % 2]
        contract = (((1,), (1,)), ((), ()))
        away = lax.dot_general(rel[pl.ds(rows_half, rows_half)], w, contract,
                               preferred_element_type=F32)
        send_bufs[0][j] = away.astype(BF16).reshape(groups // 2, out_rows, kt)
        copy_of(0, j, dims[plan[0][0]][0]).start()
        home = lax.dot_general(rel[pl.ds(0, rows_half)], w, contract, preferred_element_type=F32)
        keeps[0][j % keeps[0].shape[0]] = home.reshape(groups // 2, out_rows, kt)

    def forward(stage, j, plan):
        copy_of(stage - 1, j, dims[plan[stage - 1][0]][0]).wait_recv()
        slot = j % keeps[stage - 1].shape[0]
        if stage == nd:
            total = keeps[stage - 1][slot, 0] + recv_bufs[stage - 1][j, 0].astype(F32)
            block = xor(base, j // per_block, seq_count)
            column = pl.multiple_of(block * row_block + (j % per_block) * kt, kt)
            out[:, pl.ds(column, kt)] = total
            return
        d, sent, kept = plan[stage]
        for k, i in enumerate(sent):
            total = keeps[stage - 1][slot, i] + recv_bufs[stage - 1][j, i].astype(F32)
            send_bufs[stage][j, k] = total.astype(BF16)
        copy_of(stage, j, dims[d][0]).start()
        here = j % keeps[stage].shape[0]
        for k, i in enumerate(kept):
            keeps[stage][here, k] = keeps[stage - 1][slot, i] + recv_bufs[stage - 1][j, i].astype(F32)

    delays = [0] + [1 + lag * s for s in range(nd)]
    steps = n_tiles + delays[-1]

    def step(i, carry):
        for parity in range(2):
            now = i * 2 + parity

            @pl.when(now < n_tiles)
            def _():
                multiply(now, plans[parity])

            for stage in range(1, nd + 1):
                j = now - delays[stage]
                plan = plans[(parity - delays[stage]) % 2]

                @pl.when((j >= 0) & (j < n_tiles))
                def _():
                    forward(stage, j, plan)
        return carry

    lax.fori_loop(0, (steps + 1) // 2, step, 0)

    def drain(j, carry):
        for stage in range(nd):
            copy_of(stage, j, dims[0][0]).wait_send()
        return carry

    lax.fori_loop(0, n_tiles, drain, 0)


def project_back(seq_count, head_parts, back, gathered):
    groups, out_rows, depth = back.shape
    row_block = gathered.shape[1]
    kt = row_block // 2
    n_tiles = seq_count * 2
    lag = 3
    nd = len(bits_below(head_parts)) + 1
    sizes = [groups >> (s + 1) for s in range(nd)]
    return pl.pallas_call(
        functools.partial(reduce_kernel, seq_count, head_parts, kt, lag),
        name="project_back",
        out_shape=jax.ShapeDtypeStruct((out_rows, seq_count * row_block), F32),
        in_specs=[pl.BlockSpec(memory_space=pltpu.VMEM), pl.BlockSpec(memory_space=pl.ANY)],
        out_specs=pl.BlockSpec(memory_space=pltpu.VMEM),
        scratch_shapes=[
            pltpu.VMEM((groups * out_rows, depth), BF16),
            pltpu.VMEM((2, kt, depth), BF16),
            *[pltpu.VMEM((2 if s == 0 else lag + 1, n, out_rows, kt), F32)
              for s, n in enumerate(sizes)],
            *[pltpu.VMEM((n_tiles, n, out_rows, kt), BF16) for n in sizes],
            *[pltpu.VMEM((n_tiles, n, out_rows, kt), BF16) for n in sizes],
            pltpu.SemaphoreType.DMA((2,)),
            pltpu.SemaphoreType.DMA((nd, n_tiles)),
            pltpu.SemaphoreType.DMA((nd, n_tiles)),
        ],
        compiler_params=pltpu.CompilerParams(
            collective_id=1, has_side_effects=True, vmem_limit_bytes=VMEM_LIMIT
        ),
    )(back, gathered)


def on_device(seq_count, head_parts, hidden, w_query, w_key, w_value, cotangent):
    gathered, back = layer(seq_count, head_parts, hidden, w_query, w_key, w_value, cotangent)
    groups = 2 * head_parts
    back = back.reshape(groups, hidden.shape[0] // head_parts, back.shape[2])
    input_grad = project_back(seq_count, head_parts, back, gathered)
    factor = lax.rsqrt(jnp.mean(input_grad * input_grad, axis=-1, keepdims=True) + STEP_EPS)
    return jnp.tanh(input_grad * factor)


def solution(mesh):
    def body(*args):
        return on_device(mesh.shape["seq"], mesh.shape["head"], *args)

    return jax.shard_map(
        body,
        mesh=mesh,
        in_specs=(
            P("seq", None),
            P("seq", "head"),
            P("seq", "head"),
            P("seq", "head"),
            P("seq", "head"),
        ),
        out_specs=P(("seq", "head"), None),
        check_vma=False,
    )
```

```python
import functools

import jax
import jax.numpy as jnp
from jax import lax
from jax.experimental import pallas as pl
from jax.experimental.pallas import tpu as pltpu
from jax.sharding import PartitionSpec as P

DH = 128
NORM_EPS = 1e-05
STEP_EPS = 1e-06


F32 = jnp.float32
BF16 = jnp.bfloat16
MESH = pl.DeviceIdType.MESH
VMEM_LIMIT = 64000 * 1024
ROW_CUTS = 2
LAST_CUTS = (2, 1, 1)
AHEAD = 2
HELD_BACK = (2, 2)
TOP_GAPS = (4, 13)
TOKEN_CUTS = 4
CATCH_UP = 2
UNROLL = 1
TILE_CUTS = 2
LAG = 3


def silu_slope(preact):
    sigmoid = jax.nn.sigmoid(preact)
    return sigmoid * (1.0 + preact * (1.0 - sigmoid))


def flip(index, mask):
    bit = 1
    while bit <= mask:
        if mask & bit:
            index = index + bit * (1 - 2 * ((index // bit) % 2))
        bit *= 2
    return index


def xor(left, right, size):
    total, bit = 0, 1
    while bit < size:
        total = total + bit * ((left // bit + right // bit) % 2)
        bit *= 2
    return total


def bits_below(top):
    masks, bit = [], 1
    while bit < top:
        masks.append(bit)
        bit *= 2
    return masks


def cut_pieces(row_block, n_chunks):
    pieces = []
    for ch in range(n_chunks):
        for proj in range(3):
            last = ch == n_chunks - 1 and proj == 2
            row = 0
            for share in LAST_CUTS if last else (2,) * ROW_CUTS:
                rows = row_block // ROW_CUTS // 2 * share
                pieces.append((proj, ch, row, rows))
                row += rows
    return pieces


def greet(partners):
    barrier = pltpu.get_barrier_semaphore()
    for where in partners:
        pl.semaphore_signal(barrier, inc=1, device_id=where, device_id_type=MESH)
    pl.semaphore_wait(barrier, len(partners))


def layer_kernel(seq_count, head_parts, hidden, w_key, w_value, w_query, cot,
                 gathered, back, tokens, own, stage, pre, act, partial, grads, cot_rows,
                 outside, total, low_send, low_recv, top_send, top_recv,
                 w_send, w_recv, tok_send, tok_recv, cot_sems, local, fetch,
                 low_sems, top_sems):
    seat = lax.axis_index("seq")
    lane = lax.axis_index("head")
    tok_rows, _ = hidden.shape
    row_block, col_width = w_key.shape
    half = col_width // 2
    _, col_piece = stage.shape[1:]
    top, pair = seq_count // 2, seq_count // 4
    bit = (seat // pair) % 2
    low_masks = bits_below(pair)
    far_masks = (top | pair, top, pair)
    head_masks = bits_below(head_parts)
    share = tok_rows // head_parts
    weights = (w_key, w_value, w_query)
    n_chunks = half // col_piece
    chunk_heads = col_piece // DH
    pieces = cut_pieces(row_block, n_chunks)

    def seq_id(mask):
        return (flip(seat, mask), lane)

    def head_id(mask):
        return (seat, flip(lane, mask))

    greet([seq_id(m) for m in far_masks] + [seq_id(m) for m in low_masks]
          + [head_id(m) for m in head_masks])

    def remote(src, dst, send, recv, where):
        return pltpu.make_async_remote_copy(
            src_ref=src, dst_ref=dst, send_sem=send, recv_sem=recv,
            device_id=where, device_id_type=MESH,
        )

    sends = []

    def start(copy):
        copy.start()
        sends.append(copy)
        return copy


    def held(mask, p):
        proj, ch, row, rows = pieces[p]
        return gathered.at[
            mask, pl.ds(row, rows), pl.ds(proj * half + ch * col_piece, col_piece)
        ]

    def first_hop(mask, p):
        proj, ch, row, rows = pieces[p]
        side = 1 - bit if mask & pair else bit
        column = pl.multiple_of(side * half + ch * col_piece, col_piece)
        src = weights[proj].at[pl.ds(row, rows), pl.ds(column, col_piece)]
        return remote(src, held(mask, p), w_send.at[mask, p], w_recv.at[mask, p], seq_id(mask))

    def later_hop(mask, low, p):
        return remote(held(mask, p), held(mask | low, p), w_send.at[mask | low, p],
                      w_recv.at[mask | low, p], seq_id(low))

    arrived = set()

    def ensure(mask, p):
        if (mask, p) not in arrived:
            arrived.add((mask, p))
            here = held(mask, p)
            remote(here, here, w_send.at[mask, p], w_recv.at[mask, p], seq_id(pair)).wait_recv()

    def spread(base, p):
        for low in low_masks:
            for sub in range(low):
                if base | sub:
                    ensure(base | sub, p)
                    start(later_hop(base | sub, low, p))


    slab = share // TOKEN_CUTS
    hops = list(reversed(head_masks))

    def tok_block(index, who, cut):
        row = pl.multiple_of(who * share + cut * slab, slab)
        return tokens.at[index, pl.ds(row, slab)]

    def token_first(cut):
        row = pl.multiple_of(lane * share + cut * slab, slab)
        return remote(hidden.at[pl.ds(row, slab)], tok_block(bit, lane, cut),
                      tok_send.at[cut, 0], tok_recv.at[cut, 0], seq_id(pair))

    flights = {}

    def token_hop(cut, hop):
        for copy in flights[cut]:
            copy.wait_recv()
        if hop < len(hops):
            count = 2 ** hop
            held_shares = [0]
            for mask in hops[:hop]:
                held_shares = held_shares + [c ^ mask for c in held_shares]
            flights[cut] = []
            for k, sub in enumerate(held_shares):
                block = tok_block(1 - bit, flip(lane, sub), cut)
                flights[cut].append(start(remote(
                    block, block, tok_send.at[cut, count + k], tok_recv.at[cut, count + k],
                    head_id(hops[hop]))))

    side = pl.multiple_of((1 - bit) * half, half)
    cot_copy = remote(cot.at[:, pl.ds(side, half)], cot_rows.at[bit],
                      cot_sems.at[0], cot_sems.at[1], seq_id(pair))

    def issue(p):
        for mask in (top | pair, top, pair):
            start(first_hop(mask, p))
        for mask in low_masks:
            start(first_hop(mask, p))
        for cut in range(TOKEN_CUTS):
            if cut // 2 == p:
                flights[cut] = [start(token_first(cut))]
        if p == TOKEN_CUTS:
            start(cot_copy)

    issued = [0]

    def issue_to(count):
        while issued[0] < min(count, len(pieces)):
            issue(issued[0])
            issued[0] += 1

    issue_to(len(pieces) - HELD_BACK[0] if n_chunks > 1 else len(pieces))

    mine = pl.multiple_of(bit * half, half)
    own_copies = []
    for proj in range(3):
        copy = pltpu.make_async_copy(weights[proj].at[:, pl.ds(mine, half)],
                                     own.at[:, pl.ds(proj * half, half)], local.at[proj])
        copy.start()
        own_copies.append(copy)
    tok_local = pltpu.make_async_copy(hidden, tokens.at[bit], local.at[3])
    tok_local.start()
    cot_local = pltpu.make_async_copy(cot.at[:, pl.ds(mine, half)], cot_rows.at[bit], local.at[5])
    for copy in own_copies:
        copy.wait()
    own_out = pltpu.make_async_copy(own, gathered.at[0], local.at[4])
    own_out.start()
    own_out.wait()
    tok_local.wait()

    def project(p):
        proj, ch, row, rows = pieces[p]
        for mask in range(1, seq_count):
            ensure(mask, p)
        copies = []
        for mask in range(seq_count):
            copy = pltpu.make_async_copy(
                held(mask, p), stage.at[mask, pl.ds(0, rows)], fetch.at[mask])
            copy.start()
            copies.append(copy)
        for copy in copies:
            copy.wait()
        columns = pl.ds(ch * col_piece, col_piece)

        def block_dot(mask, carry):
            block = xor(seat, mask, seq_count)
            offset = pl.multiple_of(block * row_block + row, DH)
            for side in range(2):
                term = jnp.dot(tokens[side, :, pl.ds(offset, rows)], stage[mask, pl.ds(0, rows)],
                               preferred_element_type=F32)
                pre[proj, side, :, columns] += term
            return carry

        if row == 0:
            for side in range(2):
                pre[proj, side, :, columns] = jnp.zeros((tok_rows, col_piece), F32)
        lax.fori_loop(0, seq_count, block_dot, 0)


    def per_item(ch, work, first=0, past=2 * chunk_heads):
        def item(i, carry):
            head = ch * chunk_heads + i % chunk_heads
            work(i // chunk_heads, head, pl.ds(pl.multiple_of(head * DH, DH), DH))
            return carry

        lax.fori_loop(first, past, item, 0, unroll=UNROLL)

    band = tok_rows // 2

    def dot(left, right, left_dim, right_dim):
        return lax.dot_general(left, right, (((left_dim,), (right_dim,)), ((), ())),
                               preferred_element_type=F32)

    def states(side, head, cols):
        key = jax.nn.silu(pre[0, side, :, cols]).astype(BF16)
        value = pre[1, side, :, cols].astype(BF16)
        act[0, side, :, cols] = key
        act[1, side, :, cols] = value
        total[0, side, head] = dot(key, value, 0, 0)
        outside[0, side, head] = jnp.zeros((DH, DH), F32)

    def forward(side, head, cols):
        query = jax.nn.silu(pre[2, side, :, cols]).astype(BF16)
        act[2, side, :, cols] = query
        before = outside[0, side, head].astype(BF16)
        own_grad = jnp.zeros((DH, DH), F32)
        for start_row in (0, band):
            rows, past = pl.ds(start_row, band), start_row + band
            near_query = query[start_row:past]
            key, value = act[0, side, pl.ds(0, past), cols], act[1, side, pl.ds(0, past), cols]
            row = lax.broadcasted_iota(jnp.int32, (band, past), 0) + start_row
            column = lax.broadcasted_iota(jnp.int32, (band, past), 1)
            scores = jnp.where(row >= column, dot(near_query, key, 1, 1), 0.0).astype(BF16)
            attended = dot(scores, value, 1, 0) + dot(near_query, before, 1, 0)
            scale = lax.rsqrt(jnp.mean(attended * attended, axis=-1, keepdims=True) + NORM_EPS)
            normed = attended * scale
            upstream = cot_rows[side, rows, cols].astype(F32)
            grad = scale * (
                upstream - normed * jnp.mean(upstream * normed, axis=-1, keepdims=True))
            grad = grad.astype(BF16)
            grads[side, rows, cols] = grad
            own_grad += dot(near_query, grad, 0, 0)
        total[1, side, head] = own_grad
        outside[1, side, head] = jnp.zeros((DH, DH), F32)

    def to_back(proj, side, head, rows, result):
        column = pl.ds(pl.multiple_of(proj * half + head * DH, DH), DH)
        back[side, rows, column] = result.astype(BF16)

    def inner(side, head, cols):
        key, value, query = (act[i, side, :, cols] for i in range(3))
        grad = grads[side, :, cols]
        before = outside[0, side, head].astype(BF16)
        for start_row in (0, band):
            rows, past = pl.ds(start_row, band), start_row + band
            row = lax.broadcasted_iota(jnp.int32, (band, past), 0) + start_row
            column = lax.broadcasted_iota(jnp.int32, (band, past), 1)
            near = grad[start_row:past]
            grad_scores = jnp.where(row >= column, dot(near, value[:past], 1, 1), 0.0).astype(BF16)
            grad_query = dot(grad_scores, key[:past], 1, 0) + dot(near, before, 1, 1)
            to_back(2, side, head, rows, grad_query * silu_slope(pre[2, side, rows, cols]))
            key_row = lax.broadcasted_iota(jnp.int32, (band, tok_rows - start_row), 0)
            token = lax.broadcasted_iota(jnp.int32, (band, tok_rows - start_row), 1)
            turned = jnp.where(
                key_row <= token, dot(value[start_row:past], grad[start_row:], 1, 1), 0.0
            ).astype(BF16)
            partial[side, rows, cols] = dot(turned, query[start_row:], 1, 0)
            turned = jnp.where(
                key_row <= token, dot(key[start_row:past], query[start_row:], 1, 1), 0.0
            ).astype(BF16)
            pre[1, side, rows, cols] = dot(turned, grad[start_row:], 1, 0)

    def finish(side, head, cols):
        after = outside[1, side, head].astype(BF16)
        grad_key = partial[side, :, cols] + dot(act[1, side, :, cols], after, 1, 1)
        grad_value = pre[1, side, :, cols] + dot(act[0, side, :, cols], after, 1, 0)
        rows = pl.ds(0, tok_rows)
        to_back(0, side, head, rows, grad_key * silu_slope(pre[0, side, :, cols]))
        to_back(1, side, head, rows, grad_value)


    def heads_of(ch):
        return range(ch * chunk_heads, (ch + 1) * chunk_heads)

    def low_copy(kind, ch, i):
        return remote(low_send.at[kind, ch, i], low_recv.at[kind, ch, i],
                      low_sems.at[0, kind, ch, i], low_sems.at[1, kind, ch, i],
                      seq_id(low_masks[i]))

    def top_copy(kind, ch):
        return remote(top_send.at[kind, ch], top_recv.at[kind, ch],
                      top_sems.at[0, kind, ch], top_sems.at[1, kind, ch], seq_id(top))

    def scan_send(kind, ch, i):
        for side in range(2):
            for k, head in enumerate(heads_of(ch)):
                low_send[kind, ch, i, side, k] = total[kind, side, head].astype(BF16)
        start(low_copy(kind, ch, i))

    def scan_low(kind, ch):
        for i, low in enumerate(low_masks):
            low_copy(kind, ch, i).wait_recv()
            wanted = (seat // low) % 2 == 1 - kind
            for side in range(2):
                for k, head in enumerate(heads_of(ch)):
                    other = low_recv[kind, ch, i, side, k].astype(F32)
                    outside[kind, side, head] += jnp.where(wanted, other, 0.0)
                    total[kind, side, head] += other
            if i + 1 < len(low_masks):
                scan_send(kind, ch, i + 1)
        for k, head in enumerate(heads_of(ch)):
            outside[kind, 1 - kind, head] += total[kind, kind, head]
            whole = total[kind, 0, head] + total[kind, 1, head]
            top_send[kind, ch, k] = whole.astype(BF16)
        start(top_copy(kind, ch))

    def scan_top(kind, ch):
        top_copy(kind, ch).wait_recv()
        wanted = (seat // top) % 2 == 1 - kind
        for k, head in enumerate(heads_of(ch)):
            other = jnp.where(wanted, top_recv[kind, ch, k].astype(F32), 0.0)
            for side in range(2):
                outside[kind, side, head] += other

    def stage_states(ch):
        per_item(ch, states)
        scan_send(0, ch, 0)

    def stage_forward(ch):
        per_item(ch, forward)
        scan_send(1, ch, 0)

    chain = (
        (stage_states, 2, 0),
        (lambda ch: scan_low(0, ch), 2, 1),
        (lambda ch: scan_top(0, ch), 2, TOP_GAPS[0]),
        (stage_forward, 3, 0),
        (lambda ch: per_item(ch, inner, 0, chunk_heads), 3, 0),
        (lambda ch: scan_low(1, ch), 3, 0),
        (lambda ch: per_item(ch, inner, chunk_heads), 3, 1),
        (lambda ch: scan_top(1, ch), 3, TOP_GAPS[1]),
        (lambda ch: per_item(ch, finish), 3, 0),
    )
    place = [0] * n_chunks
    last_step = [0] * n_chunks
    projected = [0] * n_chunks
    cot_here = []

    def advance(p, final):
        moved = True
        while moved:
            moved = False
            for ch in range(n_chunks):
                if place[ch] == len(chain):
                    continue
                work, projs, gap = chain[place[ch]]
                if projected[ch] < projs * row_block or not (final or p >= last_step[ch] + gap):
                    continue
                if work is stage_forward and not cot_here:
                    cot_here.append(True)
                    cot_copy.wait_recv()
                    cot_local.start()
                    cot_local.wait()
                work(ch)
                place[ch] += 1
                if ch == 0 and place[ch] in (2, 6):
                    issue_to(len(pieces) - HELD_BACK[1] if place[ch] == 2 else len(pieces))
                last_step[ch] = p
                moved = True

    tok_step = (TOKEN_CUTS - 1) // 2 + 1 + len(hops)
    pending = []
    for p in range(len(pieces)):
        final = p == len(pieces) - 1
        issue_to(p + AHEAD)
        for mask in (top | pair, top, pair, 0):
            spread(mask, p)
        if final:
            pending.append(p)
        for hop in range(len(hops) + 1):
            for cut in range(TOKEN_CUTS):
                due = cut // 2 + 1 + hop
                if due == p or (final and due > p):
                    token_hop(cut, hop)
        if p >= tok_step or final:
            count = len(pending) if final else CATCH_UP
            for q in pending[:count]:
                project(q)
                projected[pieces[q][1]] += pieces[q][3]
                if final:
                    advance(p, True)
            pending = pending[count:]
            advance(p, final)
        pending.append(p)
    for copy in sends:
        copy.wait_send()


def layer(seq_count, head_parts, hidden, w_query, w_key, w_value, cotangent):
    tok_rows, width = hidden.shape
    row_block, col_width = w_query.shape
    half = col_width // 2
    heads = half // DH
    col_piece = min(half, 256)
    row_piece = row_block // ROW_CUTS
    n_chunks = half // col_piece
    chunk_heads = col_piece // DH
    n_pieces = len(cut_pieces(row_block, n_chunks))
    n_low = len(bits_below(seq_count // 4))
    anyspace = pl.BlockSpec(memory_space=pl.ANY)
    dma = pltpu.SemaphoreType.DMA
    return pl.pallas_call(
        functools.partial(layer_kernel, seq_count, head_parts),
        name="layer",
        out_shape=(
            jax.ShapeDtypeStruct((seq_count, row_block, 3 * half), BF16),
            jax.ShapeDtypeStruct((2, tok_rows, 3 * half), BF16),
        ),
        in_specs=[anyspace] * 5,
        out_specs=(anyspace, pl.BlockSpec(memory_space=pltpu.VMEM)),
        scratch_shapes=[
            pltpu.VMEM((2, tok_rows, width), BF16),
            pltpu.VMEM((row_block, 3 * half), BF16),
            pltpu.VMEM((seq_count, row_piece, col_piece), BF16),
            pltpu.VMEM((3, 2, tok_rows, half), F32),
            pltpu.VMEM((3, 2, tok_rows, half), BF16),
            pltpu.VMEM((2, tok_rows, half), F32),
            pltpu.VMEM((2, tok_rows, half), BF16),
            pltpu.VMEM((2, tok_rows, half), BF16),
            pltpu.VMEM((2, 2, heads, DH, DH), F32),
            pltpu.VMEM((2, 2, heads, DH, DH), F32),
            pltpu.VMEM((2, n_chunks, n_low, 2, chunk_heads, DH, DH), BF16),
            pltpu.VMEM((2, n_chunks, n_low, 2, chunk_heads, DH, DH), BF16),
            pltpu.VMEM((2, n_chunks, chunk_heads, DH, DH), BF16),
            pltpu.VMEM((2, n_chunks, chunk_heads, DH, DH), BF16),
            dma((seq_count, n_pieces)),
            dma((seq_count, n_pieces)),
            dma((TOKEN_CUTS, head_parts)),
            dma((TOKEN_CUTS, head_parts)),
            dma((2,)),
            dma((6,)),
            dma((seq_count,)),
            dma((2, 2, n_chunks, n_low)),
            dma((2, 2, n_chunks)),
        ],
        compiler_params=pltpu.CompilerParams(
            collective_id=0, has_side_effects=True, vmem_limit_bytes=VMEM_LIMIT
        ),
    )(hidden, w_key, w_value, w_query, cotangent)


def reduce_kernel(seq_count, head_parts, kt, lag, back, gathered, out, factor, *scratch):
    seat = lax.axis_index("seq")
    lane = lax.axis_index("head")
    out_rows = back.shape[1]
    row_block, _ = gathered.shape[1:]
    per_block = row_block // kt
    n_tiles = seq_count * per_block
    pair = seq_count // 4
    bit = (seat // pair) % 2
    head_masks = bits_below(head_parts)
    nd = len(head_masks) + 1
    groups = 2 ** nd
    dims = [((seat, flip(lane, m)), nd - 1 - k) for k, m in enumerate(head_masks)]
    dims.append(((flip(seat, pair), lane), 0))
    orders = (
        list(range(nd)),
        [0, nd - 1] + list(range(1, nd - 1)),
    )
    rel, w_slots = scratch[0], scratch[1]
    keeps = scratch[2:2 + nd]
    send_bufs = scratch[2 + nd:2 + 2 * nd]
    recv_bufs = scratch[2 + 2 * nd:2 + 3 * nd]
    squares, w_sem, send_sem, recv_sem = scratch[2 + 3 * nd:]

    greet([where for where, _ in dims])

    base = seat - bit * pair

    def fetch(j):
        block = xor(j // per_block, bit * pair, seq_count)
        row = pl.multiple_of((j % per_block) * kt, kt)
        return pltpu.make_async_copy(
            gathered.at[block, pl.ds(row, kt)], w_slots.at[j % 2], w_sem.at[j % 2])

    fetch(0).start()
    squares[...] = jnp.zeros_like(squares)
    for g in range(groups):
        far_side = g % 2
        who = lane
        for k, m in enumerate(head_masks):
            if (g >> (nd - 1 - k)) & 1:
                who = flip(who, m)
        side = flip(bit, 1) if far_side else bit
        rel[pl.ds(g * out_rows, out_rows)] = back[side * head_parts + who]

    plans = []
    for order in orders:
        plan, current = [], list(range(groups))
        for d in order:
            place = dims[d][1]
            sent = [i for i, g in enumerate(current) if (g >> place) & 1]
            kept = [i for i, g in enumerate(current) if not (g >> place) & 1]
            plan.append((d, sent, kept))
            current = [current[i] for i in kept]
        plans.append(plan)

    def copy_of(stage, tile, where):
        return pltpu.make_async_remote_copy(
            src_ref=send_bufs[stage].at[tile], dst_ref=recv_bufs[stage].at[tile],
            send_sem=send_sem.at[stage, tile], recv_sem=recv_sem.at[stage, tile],
            device_id=where, device_id_type=MESH)

    rows_half = groups // 2 * out_rows

    def multiply(j, plan):
        fetch(j).wait()

        @pl.when(j + 1 < n_tiles)
        def _():
            fetch(j + 1).start()

        w = w_slots[j % 2]
        contract = (((1,), (1,)), ((), ()))
        away = lax.dot_general(rel[pl.ds(rows_half, rows_half)], w, contract,
                               preferred_element_type=F32)
        send_bufs[0][j] = away.astype(BF16).reshape(groups // 2, out_rows, kt)
        copy_of(0, j, dims[plan[0][0]][0]).start()
        home = lax.dot_general(rel[pl.ds(0, rows_half)], w, contract, preferred_element_type=F32)
        keeps[0][j % keeps[0].shape[0]] = home.reshape(groups // 2, out_rows, kt)

    def forward(stage, j, plan):
        copy_of(stage - 1, j, dims[plan[stage - 1][0]][0]).wait_recv()
        slot = j % keeps[stage - 1].shape[0]
        if stage == nd:
            total = keeps[stage - 1][slot, 0] + recv_bufs[stage - 1][j, 0].astype(F32)
            block = xor(base, j // per_block, seq_count)
            column = pl.multiple_of(block * row_block + (j % per_block) * kt, kt)
            out[:, pl.ds(column, kt)] = total
            for k in range(kt // DH):
                squares[...] += total[:, k * DH:(k + 1) * DH] * total[:, k * DH:(k + 1) * DH]
            return
        d, sent, kept = plan[stage]
        for k, i in enumerate(sent):
            total = keeps[stage - 1][slot, i] + recv_bufs[stage - 1][j, i].astype(F32)
            send_bufs[stage][j, k] = total.astype(BF16)
        copy_of(stage, j, dims[d][0]).start()
        here = j % keeps[stage].shape[0]
        for k, i in enumerate(kept):
            keeps[stage][here, k] = keeps[stage - 1][slot, i] + recv_bufs[stage - 1][j, i].astype(F32)

    delays = [0] + [1 + lag * s for s in range(nd)]
    steps = n_tiles + delays[-1]

    def step(i, carry):
        for parity in range(2):
            now = i * 2 + parity

            @pl.when(now < n_tiles)
            def _():
                multiply(now, plans[parity])

            for stage in range(1, nd + 1):
                j = now - delays[stage]
                plan = plans[(parity - delays[stage]) % 2]

                @pl.when((j >= 0) & (j < n_tiles))
                def _():
                    forward(stage, j, plan)
        return carry

    lax.fori_loop(0, (steps + 1) // 2, step, 0)

    mean = jnp.sum(squares[...], axis=-1, keepdims=True) / out.shape[1]
    factor[...] = jnp.broadcast_to(lax.rsqrt(mean + STEP_EPS), factor.shape)

    def drain(j, carry):
        for stage in range(nd):
            copy_of(stage, j, dims[0][0]).wait_send()
        return carry

    lax.fori_loop(0, n_tiles, drain, 0)


def project_back(seq_count, head_parts, back, gathered):
    groups, out_rows, depth = back.shape
    row_block = gathered.shape[1]
    kt = row_block // TILE_CUTS
    n_tiles = seq_count * TILE_CUTS
    lag = LAG
    nd = len(bits_below(head_parts)) + 1
    sizes = [groups >> (s + 1) for s in range(nd)]
    return pl.pallas_call(
        functools.partial(reduce_kernel, seq_count, head_parts, kt, lag),
        name="project_back",
        out_shape=(
            jax.ShapeDtypeStruct((out_rows, seq_count * row_block), F32),
            jax.ShapeDtypeStruct((out_rows, DH), F32),
        ),
        in_specs=[pl.BlockSpec(memory_space=pltpu.VMEM), pl.BlockSpec(memory_space=pl.ANY)],
        out_specs=(pl.BlockSpec(memory_space=pltpu.VMEM),) * 2,
        scratch_shapes=[
            pltpu.VMEM((groups * out_rows, depth), BF16),
            pltpu.VMEM((2, kt, depth), BF16),
            *[pltpu.VMEM((2 if s == 0 else lag + 1, n, out_rows, kt), F32)
              for s, n in enumerate(sizes)],
            *[pltpu.VMEM((n_tiles, n, out_rows, kt), BF16) for n in sizes],
            *[pltpu.VMEM((n_tiles, n, out_rows, kt), BF16) for n in sizes],
            pltpu.VMEM((out_rows, DH), F32),
            pltpu.SemaphoreType.DMA((2,)),
            pltpu.SemaphoreType.DMA((nd, n_tiles)),
            pltpu.SemaphoreType.DMA((nd, n_tiles)),
        ],
        compiler_params=pltpu.CompilerParams(
            collective_id=1, has_side_effects=True, vmem_limit_bytes=VMEM_LIMIT
        ),
    )(back, gathered)


def on_device(seq_count, head_parts, hidden, w_query, w_key, w_value, cotangent):
    gathered, back = layer(seq_count, head_parts, hidden, w_query, w_key, w_value, cotangent)
    groups = 2 * head_parts
    back = back.reshape(groups, hidden.shape[0] // head_parts, back.shape[2])
    input_grad, factor = project_back(seq_count, head_parts, back, gathered)
    return jnp.tanh(input_grad * factor[:, :1])


def solution(mesh):
    def body(*args):
        return on_device(mesh.shape["seq"], mesh.shape["head"], *args)

    return jax.shard_map(
        body,
        mesh=mesh,
        in_specs=(
            P("seq", None),
            P("seq", "head"),
            P("seq", "head"),
            P("seq", "head"),
            P("seq", "head"),
        ),
        out_specs=P(("seq", "head"), None),
        check_vma=False,
    )
```

```python
import functools

import jax
import jax.numpy as jnp
from jax import lax
from jax.experimental import pallas as pl
from jax.experimental.pallas import tpu as pltpu
from jax.sharding import PartitionSpec as P

DH = 128
NORM_EPS = 1e-05
STEP_EPS = 1e-06


F32 = jnp.float32
BF16 = jnp.bfloat16
MESH = pl.DeviceIdType.MESH
VMEM_LIMIT = 64000 * 1024
ROW_CUTS = 2
LAST_CUTS = (2, 1, 1)
AHEAD = 2
HELD_BACK = (2, 2)
TOP_GAPS = (4, 13)
TOKEN_CUTS = 4
CATCH_UP = 2
UNROLL = 1
TILE_CUTS = 2
LAG = 3
OUT_SLOTS = 4


def silu_slope(preact):
    sigmoid = jax.nn.sigmoid(preact)
    return sigmoid * (1.0 + preact * (1.0 - sigmoid))


def flip(index, mask):
    bit = 1
    while bit <= mask:
        if mask & bit:
            index = index + bit * (1 - 2 * ((index // bit) % 2))
        bit *= 2
    return index


def xor(left, right, size):
    total, bit = 0, 1
    while bit < size:
        total = total + bit * ((left // bit + right // bit) % 2)
        bit *= 2
    return total


def bits_below(top):
    masks, bit = [], 1
    while bit < top:
        masks.append(bit)
        bit *= 2
    return masks


def cut_pieces(row_block, n_chunks):
    pieces = []
    for ch in range(n_chunks):
        for proj in range(3):
            last = ch == n_chunks - 1 and proj == 2
            row = 0
            for share in LAST_CUTS if last else (2,) * ROW_CUTS:
                rows = row_block // ROW_CUTS // 2 * share
                pieces.append((proj, ch, row, rows))
                row += rows
    return pieces


def greet(partners):
    barrier = pltpu.get_barrier_semaphore()
    for where in partners:
        pl.semaphore_signal(barrier, inc=1, device_id=where, device_id_type=MESH)
    pl.semaphore_wait(barrier, len(partners))


def layer_kernel(seq_count, head_parts, hidden, w_key, w_value, w_query, cot,
                 gathered, back_out, tokens, own, stage, pre, act, partial, grads, cot_rows,
                 outside, total, low_send, low_recv, top_send, top_recv, back,
                 w_send, w_recv, tok_send, tok_recv, cot_sems, local, fetch,
                 low_sems, top_sems, back_sems):
    seat = lax.axis_index("seq")
    lane = lax.axis_index("head")
    tok_rows, _ = hidden.shape
    row_block, col_width = w_key.shape
    half = col_width // 2
    _, col_piece = stage.shape[1:]
    top, pair = seq_count // 2, seq_count // 4
    bit = (seat // pair) % 2
    low_masks = bits_below(pair)
    far_masks = (top | pair, top, pair)
    head_masks = bits_below(head_parts)
    share = tok_rows // head_parts
    weights = (w_key, w_value, w_query)
    n_chunks = half // col_piece
    chunk_heads = col_piece // DH
    pieces = cut_pieces(row_block, n_chunks)

    def seq_id(mask):
        return (flip(seat, mask), lane)

    def head_id(mask):
        return (seat, flip(lane, mask))

    greet([seq_id(m) for m in far_masks] + [seq_id(m) for m in low_masks]
          + [head_id(m) for m in head_masks])

    def remote(src, dst, send, recv, where):
        return pltpu.make_async_remote_copy(
            src_ref=src, dst_ref=dst, send_sem=send, recv_sem=recv,
            device_id=where, device_id_type=MESH,
        )

    sends = []

    def start(copy):
        copy.start()
        sends.append(copy)
        return copy


    def held(mask, p):
        proj, ch, row, rows = pieces[p]
        return gathered.at[
            mask, pl.ds(row, rows), pl.ds(proj * half + ch * col_piece, col_piece)
        ]

    def first_hop(mask, p):
        proj, ch, row, rows = pieces[p]
        side = 1 - bit if mask & pair else bit
        column = pl.multiple_of(side * half + ch * col_piece, col_piece)
        src = weights[proj].at[pl.ds(row, rows), pl.ds(column, col_piece)]
        return remote(src, held(mask, p), w_send.at[mask, p], w_recv.at[mask, p], seq_id(mask))

    def later_hop(mask, low, p):
        return remote(held(mask, p), held(mask | low, p), w_send.at[mask | low, p],
                      w_recv.at[mask | low, p], seq_id(low))

    arrived = set()

    def ensure(mask, p):
        if (mask, p) not in arrived:
            arrived.add((mask, p))
            here = held(mask, p)
            remote(here, here, w_send.at[mask, p], w_recv.at[mask, p], seq_id(pair)).wait_recv()

    def spread(base, p):
        for low in low_masks:
            for sub in range(low):
                if base | sub:
                    ensure(base | sub, p)
                    start(later_hop(base | sub, low, p))


    slab = share // TOKEN_CUTS
    hops = list(reversed(head_masks))

    def tok_block(index, who, cut):
        row = pl.multiple_of(who * share + cut * slab, slab)
        return tokens.at[index, pl.ds(row, slab)]

    def token_first(cut):
        row = pl.multiple_of(lane * share + cut * slab, slab)
        return remote(hidden.at[pl.ds(row, slab)], tok_block(bit, lane, cut),
                      tok_send.at[cut, 0], tok_recv.at[cut, 0], seq_id(pair))

    flights = {}

    def token_hop(cut, hop):
        for copy in flights[cut]:
            copy.wait_recv()
        if hop < len(hops):
            count = 2 ** hop
            held_shares = [0]
            for mask in hops[:hop]:
                held_shares = held_shares + [c ^ mask for c in held_shares]
            flights[cut] = []
            for k, sub in enumerate(held_shares):
                block = tok_block(1 - bit, flip(lane, sub), cut)
                flights[cut].append(start(remote(
                    block, block, tok_send.at[cut, count + k], tok_recv.at[cut, count + k],
                    head_id(hops[hop]))))

    side = pl.multiple_of((1 - bit) * half, half)
    cot_copy = remote(cot.at[:, pl.ds(side, half)], cot_rows.at[bit],
                      cot_sems.at[0], cot_sems.at[1], seq_id(pair))

    def issue(p):
        for mask in (top | pair, top, pair):
            start(first_hop(mask, p))
        for mask in low_masks:
            start(first_hop(mask, p))
        for cut in range(TOKEN_CUTS):
            if cut // 2 == p:
                flights[cut] = [start(token_first(cut))]
        if p == TOKEN_CUTS:
            start(cot_copy)

    issued = [0]

    def issue_to(count):
        while issued[0] < min(count, len(pieces)):
            issue(issued[0])
            issued[0] += 1

    issue_to(len(pieces) - HELD_BACK[0] if n_chunks > 1 else len(pieces))

    mine = pl.multiple_of(bit * half, half)
    own_copies = []
    for proj in range(3):
        copy = pltpu.make_async_copy(weights[proj].at[:, pl.ds(mine, half)],
                                     own.at[:, pl.ds(proj * half, half)], local.at[proj])
        copy.start()
        own_copies.append(copy)
    tok_local = pltpu.make_async_copy(hidden, tokens.at[bit], local.at[3])
    tok_local.start()
    cot_local = pltpu.make_async_copy(cot.at[:, pl.ds(mine, half)], cot_rows.at[bit], local.at[5])
    for copy in own_copies:
        copy.wait()
    own_out = pltpu.make_async_copy(own, gathered.at[0], local.at[4])
    own_out.start()
    own_out.wait()
    tok_local.wait()

    def project(p):
        proj, ch, row, rows = pieces[p]
        for mask in range(1, seq_count):
            ensure(mask, p)
        copies = []
        for mask in range(seq_count):
            copy = pltpu.make_async_copy(
                held(mask, p), stage.at[mask, pl.ds(0, rows)], fetch.at[mask])
            copy.start()
            copies.append(copy)
        for copy in copies:
            copy.wait()
        columns = pl.ds(ch * col_piece, col_piece)

        def block_dot(mask, carry):
            block = xor(seat, mask, seq_count)
            offset = pl.multiple_of(block * row_block + row, DH)
            for side in range(2):
                term = jnp.dot(tokens[side, :, pl.ds(offset, rows)], stage[mask, pl.ds(0, rows)],
                               preferred_element_type=F32)
                pre[proj, side, :, columns] += term
            return carry

        if row == 0:
            for side in range(2):
                pre[proj, side, :, columns] = jnp.zeros((tok_rows, col_piece), F32)
        lax.fori_loop(0, seq_count, block_dot, 0)


    def per_item(ch, work, first=0, past=2 * chunk_heads):
        def item(i, carry):
            head = ch * chunk_heads + i % chunk_heads
            work(i // chunk_heads, head, pl.ds(pl.multiple_of(head * DH, DH), DH))
            return carry

        lax.fori_loop(first, past, item, 0, unroll=UNROLL)

    band = tok_rows // 2

    def dot(left, right, left_dim, right_dim):
        return lax.dot_general(left, right, (((left_dim,), (right_dim,)), ((), ())),
                               preferred_element_type=F32)

    def states(side, head, cols):
        key = jax.nn.silu(pre[0, side, :, cols]).astype(BF16)
        value = pre[1, side, :, cols].astype(BF16)
        act[0, side, :, cols] = key
        act[1, side, :, cols] = value
        total[0, side, head] = dot(key, value, 0, 0)
        outside[0, side, head] = jnp.zeros((DH, DH), F32)

    def forward(side, head, cols):
        query = jax.nn.silu(pre[2, side, :, cols]).astype(BF16)
        act[2, side, :, cols] = query
        before = outside[0, side, head].astype(BF16)
        own_grad = jnp.zeros((DH, DH), F32)
        for start_row in (0, band):
            rows, past = pl.ds(start_row, band), start_row + band
            near_query = query[start_row:past]
            key, value = act[0, side, pl.ds(0, past), cols], act[1, side, pl.ds(0, past), cols]
            row = lax.broadcasted_iota(jnp.int32, (band, past), 0) + start_row
            column = lax.broadcasted_iota(jnp.int32, (band, past), 1)
            scores = jnp.where(row >= column, dot(near_query, key, 1, 1), 0.0).astype(BF16)
            attended = dot(scores, value, 1, 0) + dot(near_query, before, 1, 0)
            scale = lax.rsqrt(jnp.mean(attended * attended, axis=-1, keepdims=True) + NORM_EPS)
            normed = attended * scale
            upstream = cot_rows[side, rows, cols].astype(F32)
            grad = scale * (
                upstream - normed * jnp.mean(upstream * normed, axis=-1, keepdims=True))
            grad = grad.astype(BF16)
            grads[side, rows, cols] = grad
            own_grad += dot(near_query, grad, 0, 0)
        total[1, side, head] = own_grad
        outside[1, side, head] = jnp.zeros((DH, DH), F32)

    def to_back(proj, side, head, rows, result):
        column = pl.ds(pl.multiple_of(proj * half + head * DH, DH), DH)
        back[side, rows, column] = result.astype(BF16)

    def inner(side, head, cols):
        key, value, query = (act[i, side, :, cols] for i in range(3))
        grad = grads[side, :, cols]
        before = outside[0, side, head].astype(BF16)
        for start_row in (0, band):
            rows, past = pl.ds(start_row, band), start_row + band
            row = lax.broadcasted_iota(jnp.int32, (band, past), 0) + start_row
            column = lax.broadcasted_iota(jnp.int32, (band, past), 1)
            near = grad[start_row:past]
            grad_scores = jnp.where(row >= column, dot(near, value[:past], 1, 1), 0.0).astype(BF16)
            grad_query = dot(grad_scores, key[:past], 1, 0) + dot(near, before, 1, 1)
            to_back(2, side, head, rows, grad_query * silu_slope(pre[2, side, rows, cols]))
            key_row = lax.broadcasted_iota(jnp.int32, (band, tok_rows - start_row), 0)
            token = lax.broadcasted_iota(jnp.int32, (band, tok_rows - start_row), 1)
            turned = jnp.where(
                key_row <= token, dot(value[start_row:past], grad[start_row:], 1, 1), 0.0
            ).astype(BF16)
            partial[side, rows, cols] = dot(turned, query[start_row:], 1, 0)
            turned = jnp.where(
                key_row <= token, dot(key[start_row:past], query[start_row:], 1, 1), 0.0
            ).astype(BF16)
            pre[1, side, rows, cols] = dot(turned, grad[start_row:], 1, 0)

    def finish(side, head, cols):
        after = outside[1, side, head].astype(BF16)
        grad_key = partial[side, :, cols] + dot(act[1, side, :, cols], after, 1, 1)
        grad_value = pre[1, side, :, cols] + dot(act[0, side, :, cols], after, 1, 0)
        rows = pl.ds(0, tok_rows)
        to_back(0, side, head, rows, grad_key * silu_slope(pre[0, side, :, cols]))
        to_back(1, side, head, rows, grad_value)


    def heads_of(ch):
        return range(ch * chunk_heads, (ch + 1) * chunk_heads)

    def low_copy(kind, ch, i):
        return remote(low_send.at[kind, ch, i], low_recv.at[kind, ch, i],
                      low_sems.at[0, kind, ch, i], low_sems.at[1, kind, ch, i],
                      seq_id(low_masks[i]))

    def top_copy(kind, ch):
        return remote(top_send.at[kind, ch], top_recv.at[kind, ch],
                      top_sems.at[0, kind, ch], top_sems.at[1, kind, ch], seq_id(top))

    def scan_send(kind, ch, i):
        for side in range(2):
            for k, head in enumerate(heads_of(ch)):
                low_send[kind, ch, i, side, k] = total[kind, side, head].astype(BF16)
        start(low_copy(kind, ch, i))

    def scan_low(kind, ch):
        for i, low in enumerate(low_masks):
            low_copy(kind, ch, i).wait_recv()
            wanted = (seat // low) % 2 == 1 - kind
            for side in range(2):
                for k, head in enumerate(heads_of(ch)):
                    other = low_recv[kind, ch, i, side, k].astype(F32)
                    outside[kind, side, head] += jnp.where(wanted, other, 0.0)
                    total[kind, side, head] += other
            if i + 1 < len(low_masks):
                scan_send(kind, ch, i + 1)
        for k, head in enumerate(heads_of(ch)):
            outside[kind, 1 - kind, head] += total[kind, kind, head]
            whole = total[kind, 0, head] + total[kind, 1, head]
            top_send[kind, ch, k] = whole.astype(BF16)
        start(top_copy(kind, ch))

    def scan_top(kind, ch):
        top_copy(kind, ch).wait_recv()
        wanted = (seat // top) % 2 == 1 - kind
        for k, head in enumerate(heads_of(ch)):
            other = jnp.where(wanted, top_recv[kind, ch, k].astype(F32), 0.0)
            for side in range(2):
                outside[kind, side, head] += other

    def stage_states(ch):
        per_item(ch, states)
        scan_send(0, ch, 0)

    def stage_forward(ch):
        per_item(ch, forward)
        scan_send(1, ch, 0)

    back_copies = []

    def stage_finish(ch):
        per_item(ch, finish)
        for proj in range(3):
            columns = pl.ds(proj * half + ch * col_piece, col_piece)
            copy = pltpu.make_async_copy(
                back.at[:, :, columns], back_out.at[:, :, columns], back_sems.at[proj, ch])
            copy.start()
            back_copies.append(copy)

    chain = (
        (stage_states, 2, 0),
        (lambda ch: scan_low(0, ch), 2, 1),
        (lambda ch: scan_top(0, ch), 2, TOP_GAPS[0]),
        (stage_forward, 3, 0),
        (lambda ch: per_item(ch, inner, 0, chunk_heads), 3, 0),
        (lambda ch: scan_low(1, ch), 3, 0),
        (lambda ch: per_item(ch, inner, chunk_heads), 3, 1),
        (lambda ch: scan_top(1, ch), 3, TOP_GAPS[1]),
        (stage_finish, 3, 0),
    )
    place = [0] * n_chunks
    last_step = [0] * n_chunks
    projected = [0] * n_chunks
    cot_here = []

    def advance(p, final):
        moved = True
        while moved:
            moved = False
            for ch in range(n_chunks):
                if place[ch] == len(chain):
                    continue
                work, projs, gap = chain[place[ch]]
                if projected[ch] < projs * row_block or not (final or p >= last_step[ch] + gap):
                    continue
                if work is stage_forward and not cot_here:
                    cot_here.append(True)
                    cot_copy.wait_recv()
                    cot_local.start()
                    cot_local.wait()
                work(ch)
                place[ch] += 1
                if ch == 0 and place[ch] in (2, 6):
                    issue_to(len(pieces) - HELD_BACK[1] if place[ch] == 2 else len(pieces))
                last_step[ch] = p
                moved = True

    tok_step = (TOKEN_CUTS - 1) // 2 + 1 + len(hops)
    pending = []
    for p in range(len(pieces)):
        final = p == len(pieces) - 1
        issue_to(p + AHEAD)
        for mask in (top | pair, top, pair, 0):
            spread(mask, p)
        if final:
            pending.append(p)
        for hop in range(len(hops) + 1):
            for cut in range(TOKEN_CUTS):
                due = cut // 2 + 1 + hop
                if due == p or (final and due > p):
                    token_hop(cut, hop)
        if p >= tok_step or final:
            count = len(pending) if final else CATCH_UP
            for q in pending[:count]:
                project(q)
                projected[pieces[q][1]] += pieces[q][3]
                if final:
                    advance(p, True)
            pending = pending[count:]
            advance(p, final)
        pending.append(p)
    for copy in sends:
        copy.wait_send()
    for copy in back_copies:
        copy.wait()


def layer(seq_count, head_parts, hidden, w_query, w_key, w_value, cotangent):
    tok_rows, width = hidden.shape
    row_block, col_width = w_query.shape
    half = col_width // 2
    heads = half // DH
    col_piece = min(half, 256)
    row_piece = row_block // ROW_CUTS
    n_chunks = half // col_piece
    chunk_heads = col_piece // DH
    n_pieces = len(cut_pieces(row_block, n_chunks))
    n_low = len(bits_below(seq_count // 4))
    anyspace = pl.BlockSpec(memory_space=pl.ANY)
    dma = pltpu.SemaphoreType.DMA
    return pl.pallas_call(
        functools.partial(layer_kernel, seq_count, head_parts),
        name="layer",
        out_shape=(
            jax.ShapeDtypeStruct((seq_count, row_block, 3 * half), BF16),
            jax.ShapeDtypeStruct((2, tok_rows, 3 * half), BF16),
        ),
        in_specs=[anyspace] * 5,
        out_specs=(anyspace, anyspace),
        scratch_shapes=[
            pltpu.VMEM((2, tok_rows, width), BF16),
            pltpu.VMEM((row_block, 3 * half), BF16),
            pltpu.VMEM((seq_count, row_piece, col_piece), BF16),
            pltpu.VMEM((3, 2, tok_rows, half), F32),
            pltpu.VMEM((3, 2, tok_rows, half), BF16),
            pltpu.VMEM((2, tok_rows, half), F32),
            pltpu.VMEM((2, tok_rows, half), BF16),
            pltpu.VMEM((2, tok_rows, half), BF16),
            pltpu.VMEM((2, 2, heads, DH, DH), F32),
            pltpu.VMEM((2, 2, heads, DH, DH), F32),
            pltpu.VMEM((2, n_chunks, n_low, 2, chunk_heads, DH, DH), BF16),
            pltpu.VMEM((2, n_chunks, n_low, 2, chunk_heads, DH, DH), BF16),
            pltpu.VMEM((2, n_chunks, chunk_heads, DH, DH), BF16),
            pltpu.VMEM((2, n_chunks, chunk_heads, DH, DH), BF16),
            pltpu.VMEM((2, tok_rows, 3 * half), BF16),
            dma((seq_count, n_pieces)),
            dma((seq_count, n_pieces)),
            dma((TOKEN_CUTS, head_parts)),
            dma((TOKEN_CUTS, head_parts)),
            dma((2,)),
            dma((6,)),
            dma((seq_count,)),
            dma((2, 2, n_chunks, n_low)),
            dma((2, 2, n_chunks)),
            dma((3, n_chunks)),
        ],
        compiler_params=pltpu.CompilerParams(
            collective_id=0, has_side_effects=True, vmem_limit_bytes=VMEM_LIMIT
        ),
    )(hidden, w_key, w_value, w_query, cotangent)


def reduce_kernel(seq_count, head_parts, kt, lag, back, gathered, out, factor, *scratch):
    seat = lax.axis_index("seq")
    lane = lax.axis_index("head")
    out_rows = back.shape[1]
    row_block, _ = gathered.shape[1:]
    per_block = row_block // kt
    n_tiles = seq_count * per_block
    pair = seq_count // 4
    bit = (seat // pair) % 2
    head_masks = bits_below(head_parts)
    nd = len(head_masks) + 1
    groups = 2 ** nd
    dims = [((seat, flip(lane, m)), nd - 1 - k) for k, m in enumerate(head_masks)]
    dims.append(((flip(seat, pair), lane), 0))
    orders = (
        list(range(nd)),
        [0, nd - 1] + list(range(1, nd - 1)),
    )
    rel, w_slots = scratch[0], scratch[1]
    keeps = scratch[2:2 + nd]
    send_bufs = scratch[2 + nd:2 + 2 * nd]
    recv_bufs = scratch[2 + 2 * nd:2 + 3 * nd]
    squares, out_slots, w_sem, rel_sem, out_sem, send_sem, recv_sem = scratch[2 + 3 * nd:]

    base = seat - bit * pair

    def fetch(j):
        block = xor(j // per_block, bit * pair, seq_count)
        row = pl.multiple_of((j % per_block) * kt, kt)
        return pltpu.make_async_copy(
            gathered.at[block, pl.ds(row, kt)], w_slots.at[j % 2], w_sem.at[j % 2])

    fetch(0).start()
    squares[...] = jnp.zeros_like(squares)
    rel_copies = []
    for g in range(groups):
        far_side = g % 2
        who = lane
        for k, m in enumerate(head_masks):
            if (g >> (nd - 1 - k)) & 1:
                who = flip(who, m)
        side = flip(bit, 1) if far_side else bit
        copy = pltpu.make_async_copy(
            back.at[side * head_parts + who], rel.at[pl.ds(g * out_rows, out_rows)], rel_sem.at[g])
        copy.start()
        rel_copies.append(copy)
    greet([where for where, _ in dims])
    for copy in rel_copies:
        copy.wait()

    plans = []
    for order in orders:
        plan, current = [], list(range(groups))
        for d in order:
            place = dims[d][1]
            sent = [i for i, g in enumerate(current) if (g >> place) & 1]
            kept = [i for i, g in enumerate(current) if not (g >> place) & 1]
            plan.append((d, sent, kept))
            current = [current[i] for i in kept]
        plans.append(plan)

    def copy_of(stage, tile, where):
        return pltpu.make_async_remote_copy(
            src_ref=send_bufs[stage].at[tile], dst_ref=recv_bufs[stage].at[tile],
            send_sem=send_sem.at[stage, tile], recv_sem=recv_sem.at[stage, tile],
            device_id=where, device_id_type=MESH)

    def copy_out(j):
        block = xor(base, j // per_block, seq_count)
        column = pl.multiple_of(block * row_block + (j % per_block) * kt, kt)
        return pltpu.make_async_copy(
            out_slots.at[j % OUT_SLOTS], out.at[:, pl.ds(column, kt)], out_sem.at[j % OUT_SLOTS])

    rows_half = groups // 2 * out_rows

    def multiply(j, plan):
        fetch(j).wait()

        @pl.when(j + 1 < n_tiles)
        def _():
            fetch(j + 1).start()

        w = w_slots[j % 2]
        contract = (((1,), (1,)), ((), ()))
        away = lax.dot_general(rel[pl.ds(rows_half, rows_half)], w, contract,
                               preferred_element_type=F32)
        send_bufs[0][j] = away.astype(BF16).reshape(groups // 2, out_rows, kt)
        copy_of(0, j, dims[plan[0][0]][0]).start()
        home = lax.dot_general(rel[pl.ds(0, rows_half)], w, contract, preferred_element_type=F32)
        keeps[0][j % keeps[0].shape[0]] = home.reshape(groups // 2, out_rows, kt)

    def forward(stage, j, plan):
        copy_of(stage - 1, j, dims[plan[stage - 1][0]][0]).wait_recv()
        slot = j % keeps[stage - 1].shape[0]
        if stage == nd:
            total = keeps[stage - 1][slot, 0] + recv_bufs[stage - 1][j, 0].astype(F32)

            @pl.when(j >= OUT_SLOTS)
            def _():
                copy_out(j - OUT_SLOTS).wait()

            out_slots[j % OUT_SLOTS] = total
            copy_out(j).start()
            for k in range(kt // DH):
                squares[...] += total[:, k * DH:(k + 1) * DH] * total[:, k * DH:(k + 1) * DH]
            return
        d, sent, kept = plan[stage]
        for k, i in enumerate(sent):
            total = keeps[stage - 1][slot, i] + recv_bufs[stage - 1][j, i].astype(F32)
            send_bufs[stage][j, k] = total.astype(BF16)
        copy_of(stage, j, dims[d][0]).start()
        here = j % keeps[stage].shape[0]
        for k, i in enumerate(kept):
            keeps[stage][here, k] = keeps[stage - 1][slot, i] + recv_bufs[stage - 1][j, i].astype(F32)

    delays = [0] + [1 + lag * s for s in range(nd)]
    steps = n_tiles + delays[-1]

    def step(i, carry):
        for parity in range(2):
            now = i * 2 + parity

            @pl.when(now < n_tiles)
            def _():
                multiply(now, plans[parity])

            for stage in range(1, nd + 1):
                j = now - delays[stage]
                plan = plans[(parity - delays[stage]) % 2]

                @pl.when((j >= 0) & (j < n_tiles))
                def _():
                    forward(stage, j, plan)
        return carry

    lax.fori_loop(0, (steps + 1) // 2, step, 0)

    mean = jnp.sum(squares[...], axis=-1, keepdims=True) / out.shape[1]
    factor[...] = jnp.broadcast_to(lax.rsqrt(mean + STEP_EPS), factor.shape)

    def drain(j, carry):
        for stage in range(nd):
            copy_of(stage, j, dims[0][0]).wait_send()
        return carry

    lax.fori_loop(0, n_tiles, drain, 0)
    for j in range(n_tiles - OUT_SLOTS, n_tiles):
        copy_out(j).wait()


def project_back(seq_count, head_parts, back, gathered):
    groups, out_rows, depth = back.shape
    row_block = gathered.shape[1]
    kt = row_block // TILE_CUTS
    n_tiles = seq_count * TILE_CUTS
    lag = LAG
    nd = len(bits_below(head_parts)) + 1
    sizes = [groups >> (s + 1) for s in range(nd)]
    return pl.pallas_call(
        functools.partial(reduce_kernel, seq_count, head_parts, kt, lag),
        name="project_back",
        out_shape=(
            jax.ShapeDtypeStruct((out_rows, seq_count * row_block), F32),
            jax.ShapeDtypeStruct((out_rows, DH), F32),
        ),
        in_specs=[pl.BlockSpec(memory_space=pl.ANY)] * 2,
        out_specs=(
            pl.BlockSpec(memory_space=pl.ANY), pl.BlockSpec(memory_space=pltpu.VMEM),
        ),
        scratch_shapes=[
            pltpu.VMEM((groups * out_rows, depth), BF16),
            pltpu.VMEM((2, kt, depth), BF16),
            *[pltpu.VMEM((2 if s == 0 else lag + 1, n, out_rows, kt), F32)
              for s, n in enumerate(sizes)],
            *[pltpu.VMEM((n_tiles, n, out_rows, kt), BF16) for n in sizes],
            *[pltpu.VMEM((n_tiles, n, out_rows, kt), BF16) for n in sizes],
            pltpu.VMEM((out_rows, DH), F32),
            pltpu.VMEM((OUT_SLOTS, out_rows, kt), F32),
            pltpu.SemaphoreType.DMA((2,)),
            pltpu.SemaphoreType.DMA((groups,)),
            pltpu.SemaphoreType.DMA((OUT_SLOTS,)),
            pltpu.SemaphoreType.DMA((nd, n_tiles)),
            pltpu.SemaphoreType.DMA((nd, n_tiles)),
        ],
        compiler_params=pltpu.CompilerParams(
            collective_id=1, has_side_effects=True, vmem_limit_bytes=VMEM_LIMIT
        ),
    )(back, gathered)


def on_device(seq_count, head_parts, hidden, w_query, w_key, w_value, cotangent):
    gathered, back = layer(seq_count, head_parts, hidden, w_query, w_key, w_value, cotangent)
    groups = 2 * head_parts
    back = back.reshape(groups, hidden.shape[0] // head_parts, back.shape[2])
    input_grad, factor = project_back(seq_count, head_parts, back, gathered)
    return jnp.tanh(input_grad * factor[:, :1])


def solution(mesh):
    def body(*args):
        return on_device(mesh.shape["seq"], mesh.shape["head"], *args)

    return jax.shard_map(
        body,
        mesh=mesh,
        in_specs=(
            P("seq", None),
            P("seq", "head"),
            P("seq", "head"),
            P("seq", "head"),
            P("seq", "head"),
        ),
        out_specs=P(("seq", "head"), None),
        check_vma=False,
    )
```
